256 devices in a mesh: cfg: 32 (over y, x, core), tm: 8 (over z).
Axes of the slice: x: 4, y: 4, z: 8, core: 2. Of those that a mesh axis runs over, the one named last changes fastest.
Arguments:
- targets: float32 [8192, 1024], P('cfg', 'tm'), may hold values from -6 to 6
- features: float32 [8192, 64], P('cfg'), may hold values from -6 to 6
- inv_scales: float32 [64], replicated, may hold values from 0.05 to 0.3
- noise: float32 [8192], P('cfg'), may hold values from 0.1 to 1
- time_kernel: float32 [1024, 1024], P('tm'), may hold values from -1 to 1, as said below
- block_mask: int32 [8192, 8], P('cfg', 'tm'), may hold values from 0 to 1, as said below
Outputs:
- solution_field: float32 [8192, 1024], P('cfg', 'tm')
- residual: float32 [8192, 1024], P('cfg', 'tm')
The draws below stay inside these ranges and needn't reach their ends.
Inputs may be any that keep to these rules, and one draw needn't show every extreme that they name: `block_mask`: each configuration observes one contiguous run of blocks that starts at a block of 0 to 2 and has at least one block; some runs start late and some reach the last block. `time_kernel`: symmetric positive definite, with unit diagonal.
All inputs are finite; a program needn't handle non-finite values.
Results may differ from the reference program's by a relative error of at most 0.00026.
Values sent between devices are 32-bit elements; how exact they have to be, the bound alone decides.
A program may use at most 64 MiB of HBM per device.

```python
import math
import jax
import jax.numpy as jnp
from jax import lax

F = 64
BLOCK = 128
ITERS = 2
NC = 8192
NT = 1024
NB = 8


def draw_time_kernel(key, part):
    place_key, mix_key = jax.random.split(jax.random.fold_in(key, 29))
    increments = jax.random.uniform(place_key, (NT,), jnp.float32, 0.5, 1.5)
    factor = jax.random.normal(mix_key, (NT, 2 * NT), jnp.float32)
    places = jnp.cumsum(increments)
    smooth = jnp.exp(-jnp.abs(places[:, None] - places[None, :]) / (NT / 8.0))
    rough = jnp.dot(factor, factor.T, precision=lax.Precision.HIGHEST, preferred_element_type=jnp.float32) / (2.0 * NT)
    rough = 0.5 * (rough + rough.T)
    total = 0.5 * smooth + 0.5 * rough
    inverse_root = 1.0 / jnp.sqrt(jnp.diagonal(total))
    kernel = total * inverse_root[:, None] * inverse_root[None, :]
    kernel = 0.5 * (kernel + kernel.T)
    steps = jnp.arange(NT, dtype=jnp.int32)
    on_diagonal = steps[:, None] == steps[None, :]
    return jnp.where(on_diagonal, 1.0, jnp.clip(kernel, -1.0, 1.0)).astype(jnp.float32)


def draw_block_mask(key, part):
    first_key, second_key = jax.random.split(jax.random.fold_in(key, 17))
    begin = jax.random.randint(first_key, (NC,), 0, NB // 4 + 1)
    finish = jax.random.randint(second_key, (NC,), begin + 1, NB + 1)
    finish = finish.at[0].set(NB)
    begin = begin.at[1].set(NB // 4)
    finish = finish.at[1].set(NB // 4 + 1)
    blocks = jnp.arange(NB, dtype=jnp.int32)[None, :]
    return ((blocks >= begin[:, None]) & (blocks < finish[:, None])).astype(jnp.int32)


def block_scale(rng, extent, cuts, low, top_value):
    loudness, own = 1.0, jax.random.fold_in(rng, 6)
    for position, parts in cuts:
        steps = jnp.exp(jax.random.uniform(jax.random.fold_in(own, position), (parts,), jnp.float32, low / len(cuts), top_value / len(cuts)))
        loudness = loudness * jnp.repeat(steps, extent[position] // parts).reshape([-1 if axis == position else 1 for axis in range(len(extent))])
    return loudness


def bell_draw(own_key, extent, spread, most, shards=(), kind=jnp.bfloat16):
    level = block_scale(own_key, extent, shards, -0.22, 0.18) if shards else 1.0
    array = jax.random.normal(own_key, extent, jnp.float32) * spread * level
    return jnp.minimum(jnp.maximum(array, -most), most).astype(kind)


def setup_inputs(seed: int = 0) -> dict:
    keys = jax.random.split(jax.random.key(seed), 7)
    targets = bell_draw(keys[0], (NC, NT), 1.0, 6.0, ((0, 32), (1, 8)), jnp.float32)
    features = bell_draw(keys[1], (NC, F), 1.0, 6.0, ((0, 32),), jnp.float32)
    inv_scales = jnp.clip(jnp.exp(jax.random.uniform(keys[2], (F,), jnp.float32, math.log(0.05), math.log(0.3))), 0.05, 0.3)
    noise = jnp.clip(jnp.exp(math.log(1.0) - 2.3025851 * jax.random.uniform(keys[3], (NC,), jnp.float32) ** block_scale(keys[3], (NC,), ((0, 32),), -0.2, 0.2)), 0.1, 1.0)
    time_kernel = draw_time_kernel(jax.random.fold_in(keys[6], 71), 0)
    block_mask = draw_block_mask(jax.random.fold_in(keys[6], 71), 0)
    return {"targets": targets, "features": features, "inv_scales": inv_scales, "noise": noise, "time_kernel": time_kernel, "block_mask": block_mask}


def matern(left, right):
    cross = jnp.dot(left, right.T, precision=lax.Precision.HIGHEST, preferred_element_type=jnp.float32)
    dist2 = lax.optimization_barrier(jnp.sum(left * left, axis=1))[:, None] + lax.optimization_barrier(jnp.sum(right * right, axis=1))[None, :] - 2.0 * cross
    scaled_dist = jnp.sqrt(3.0) * jnp.sqrt(jnp.maximum(dist2, 0.0))
    return (1.0 + scaled_dist) * jnp.exp(-scaled_dist)

def reference(targets, features, inv_scales, noise, time_kernel, block_mask):
    count = targets.shape[0]
    mask = jnp.repeat(block_mask.astype(jnp.float32), BLOCK, axis=1)
    scaled = features * inv_scales[None, :]
    rowblk = math.gcd(count, 512)

    def operate(field):
        masked = mask * field

        def one_block(start):
            rows = lax.dynamic_slice_in_dim(scaled, start, rowblk, 0)
            return jnp.dot(matern(rows, scaled), masked, precision=lax.Precision.HIGHEST, preferred_element_type=jnp.float32)
        starts = (jnp.arange(count // rowblk) * rowblk).astype(jnp.int32)
        mixed = lax.map(one_block, starts).reshape(count, -1)
        timed = jnp.dot(mixed, time_kernel, precision=lax.Precision.HIGHEST, preferred_element_type=jnp.float32)
        return mask * timed + noise[:, None] * field
    residual = mask * targets
    direction = residual
    solution_field = jnp.zeros_like(residual)
    norm_now = jnp.sum(residual * residual)
    for step in range(ITERS):
        image = operate(direction)
        alpha = norm_now / jnp.sum(direction * image)
        solution_field = solution_field + alpha * direction
        residual = residual - alpha * image
        norm_next = jnp.sum(residual * residual)
        direction = residual + norm_next / norm_now * direction
        norm_now = norm_next
    return (solution_field, residual)
```

```python
import math

import jax
import jax.numpy as jnp
from jax import lax
from jax.experimental import pallas as pl
from jax.experimental.pallas import tpu as pltpu
from jax.sharding import PartitionSpec as P

MESH = pl.DeviceIdType.MESH
F32, BF16 = jnp.float32, jnp.bfloat16
NY, NX, NCORE, NZ = 4, 4, 2, 8
PLANE = NY * NX * NCORE
ROWS, COLS, FEAT = 256, 128, 64
DEPTH = 384
CHUNKS = 4
NSEM = 192
UNIT = math.sqrt(3.0) * math.log2(math.e)
LN2 = math.log(2.0)


def split2(x):
    hi = x.astype(BF16)
    return hi, (x - hi.astype(F32)).astype(BF16)


def nt_dot(a, b):
    return lax.dot_general(a, b, (((1,), (1,)), ((), ())), preferred_element_type=F32)


def kernel(
    tgt, feat, isc, noise_ref, tk, bm, sol, res,
    zg, wy, fy, fx, fl, fr, kc, wb, vb, tn, p, rel, fin, nz, mk,
    arsrc, arp, arz, ss, rs, ars, arr,
):
    me, z = lax.axis_index("cfg"), lax.axis_index("tm")
    core = lax.rem(me, NCORE)
    x = lax.rem(me // NCORE, NX)
    y = me // (NCORE * NX)

    def at(yy, xx, cc):
        return ((yy * NX + xx) * NCORE + cc, z)

    right, left = at(y, lax.rem(x + 1, NX), core), at(y, lax.rem(x + NX - 1, NX), core)
    up, down = at(lax.rem(y + 1, NY), x, core), at(lax.rem(y + NY - 1, NY), x, core)
    mate = at(y, x, 1 - core)
    zup, zdown = (me, lax.rem(z + 1, NZ)), (me, lax.rem(z + NZ - 1, NZ))
    plane = [(lax.rem(me + r, PLANE), z) for r in range(1, PLANE)]
    column = [(me, lax.rem(z + r, NZ)) for r in range(1, NZ)]

    copies = []

    def copy(src, dst, dev):
        i = len(copies)
        assert i < NSEM
        d = pltpu.make_async_remote_copy(
            src_ref=src, dst_ref=dst, send_sem=ss.at[i], recv_sem=rs.at[i],
            device_id=dev, device_id_type=MESH,
        )
        copies.append(d)
        return d

    barrier = pltpu.get_barrier_semaphore()
    for dev in plane + column:
        pl.semaphore_signal(barrier, inc=1, device_id=dev, device_id_type=MESH)

    mk[...] = jnp.broadcast_to(bm[...].astype(F32), (COLS, ROWS)).T
    nz[...] = jnp.broadcast_to(noise_ref[...], (COLS, ROWS)).T
    zg[0, 0] = mk[...] * tgt[...]
    fscaled = feat[...] * (isc[...].T * UNIT)
    fy[0, 0] = fscaled
    fx[0] = fscaled

    pl.semaphore_wait(barrier, len(plane) + len(column))

    def ring4(buf, nh, fwd, back):
        d = {}
        for h in range(nh):
            d["R1", h] = copy(buf(0, h), buf(1, h), fwd)
            d["L1", h] = copy(buf(0, h), buf(3, h), back)
        for h in range(nh):
            if h < nh // 2:
                d["2", h] = copy(buf(1, h), buf(2, h), fwd)
            else:
                d["2", h] = copy(buf(3, h), buf(2, h), back)
        return d

    def y_ring(buf, nh):
        d = ring4(lambda k, h: buf(0, k, h), nh, up, down)
        for k in (0, 1, 3, 2):
            for h in range(nh):
                d["m", k, h] = copy(buf(0, k, h), buf(1, k, h), mate)
        return d

    def ring_step1(d, nh, mated):
        for h in range(nh):
            d["R1", h].wait_recv()
            if h < nh // 2:
                d["2", h].start()
            if mated:
                d["m", 1, h].start()
            d["L1", h].wait_recv()
            if h >= nh // 2:
                d["2", h].start()
            if mated:
                d["m", 3, h].start()

    def ring_step2(d, nh, mated):
        for h in range(nh):
            d["2", h].wait_recv()
            if mated:
                d["m", 2, h].start()

    def mate_wait(d, nh, k):
        for h in range(nh):
            d["m", k, h].wait_recv()

    CR = ROWS // CHUNKS

    def z_ring(it):
        d = {}
        for s in range(1, 5):
            for c in range(CHUNKS):
                sl = pl.ds(c * CR, CR)
                if s < 4 or c < CHUNKS // 2:
                    d["R", s, c] = copy(zg.at[it, s - 1, sl], zg.at[it, s, sl], zup)
                if s < 4 or c >= CHUNKS // 2:
                    d["L", s, c] = copy(zg.at[it, (9 - s) % 8, sl], zg.at[it, 8 - s, sl], zdown)
        return d

    def z_start(d, c):
        d["R", 1, c].start()
        d["L", 1, c].start()

    def z_step(d, s):
        for c in range(CHUNKS):
            for way in "RL":
                if (way, s, c) in d:
                    d[way, s, c].wait_recv()
                if (way, s + 1, c) in d:
                    d[way, s + 1, c].start()

    def plane_copies(n):
        return [
            pltpu.make_async_remote_copy(
                src_ref=arsrc.at[n, 0], dst_ref=arp.at[n, r], send_sem=ars.at[n, 0], recv_sem=arr.at[n, 0],
                device_id=dev, device_id_type=MESH,
            )
            for r, dev in enumerate(plane)
        ]

    def column_copies(n):
        return [
            pltpu.make_async_remote_copy(
                src_ref=arsrc.at[n, 1], dst_ref=arz.at[n, r], send_sem=ars.at[n, 1], recv_sem=arr.at[n, 1],
                device_id=dev, device_id_type=MESH,
            )
            for r, dev in enumerate(column)
        ]

    def whole(n, j):
        buf, dev = (arp, plane[0]) if j == 0 else (arz, column[0])
        return pltpu.make_async_remote_copy(
            src_ref=buf.at[n], dst_ref=buf.at[n], send_sem=ars.at[n, j], recv_sem=arr.at[n, j],
            device_id=dev, device_id_type=MESH,
        )

    def sum_start(n, first, second):
        arsrc[n, 0, 0:1] = jnp.sum(first, axis=0, keepdims=True)
        arsrc[n, 0, 1:2] = jnp.sum(second, axis=0, keepdims=True)
        for d in plane_copies(n):
            d.start()

    def sum_middle(n):
        whole(n, 0).wait_recv()
        arsrc[n, 1] = arsrc[n, 0] + jnp.sum(arp[n], axis=0)
        for d in column_copies(n):
            d.start()

    def sum_end(n):
        whole(n, 1).wait_recv()
        both = arsrc[n, 1] + jnp.sum(arz[n], axis=0)
        both = jnp.sum(both, axis=1, keepdims=True)
        return both[0:1], both[1:2]

    dz = z_ring(0)
    for c in range(CHUNKS):
        z_start(dz, c)
    FH = ROWS // 2
    dfx = ring4(lambda k, h: fx.at[k, :, pl.ds(h * FH, FH)], 2, right, left)
    dfy = y_ring(lambda c, k, h: fy.at[c, k, :, pl.ds(h * FH, FH)], 2)
    for h in range(2):
        for way in ("R1", "L1"):
            dfy[way, h].start()
            dfx[way, h].start()
        dfy["m", 0, h].start()

    for k in range(NZ):
        o = lax.rem(z + NZ - k, NZ)
        hi, lo = split2(tk[:, pl.ds(pl.multiple_of(o * COLS, COLS), COLS)])
        tn[0:COLS, k * COLS : (k + 1) * COLS] = hi
        tn[COLS : 2 * COLS, k * COLS : (k + 1) * COLS] = lo

    def parts(block):
        hi = block.astype(BF16).astype(F32)
        lo = (block - hi).astype(BF16).astype(F32)
        kept = hi + lo
        n = jnp.sum(kept * kept, axis=0, keepdims=True)
        n1 = n.astype(BF16).astype(F32)
        n2 = (n - n1).astype(BF16).astype(F32)
        return hi, lo, jnp.concatenate([n1, n2, n - n1 - n2], axis=0)

    pad = DEPTH - 4 * FEAT
    row = lax.broadcasted_iota(jnp.int32, (pad, ROWS), 0)

    def place(n, first):
        out = jnp.where((row >= 3 - first) & (row < 6 - first), 1.0, 0.0)
        for i in range(3):
            out = jnp.where(row == first + i, jnp.broadcast_to(n[i : i + 1], (pad, ROWS)), out)
        return out

    def build_left(k):
        hi, lo, n = parts(fx[k])
        stack = jnp.concatenate([-2.0 * hi, -2.0 * hi, -2.0 * lo, -2.0 * lo, place(n, 0)], axis=0)
        fl[k * ROWS : (k + 1) * ROWS, :] = stack.T.astype(BF16)

    def build_right(c, k):
        hi, lo, n = parts(fy[c, k])
        stack = jnp.concatenate([hi, lo, hi, lo, place(n, 3)], axis=0)
        j = c * NY + k
        fr[:, j * ROWS : (j + 1) * ROWS] = stack.astype(BF16)

    def make_kernel(c, k):
        build_right(c, k)
        j = c * NY + k
        cols = slice(j * ROWS, (j + 1) * ROWS)
        low = slice((8 + j) * ROWS, (9 + j) * ROWS)

        def one(i, carry):
            sl = pl.ds(pl.multiple_of(i * ROWS, ROWS), ROWS)
            d2 = jnp.dot(fl[sl, :], fr[:, cols], preferred_element_type=F32)
            d2 = jnp.maximum(d2, 1e-30)
            u = d2 * lax.rsqrt(d2)
            value = (1.0 + LN2 * u) * jnp.exp2(-u)
            hi, lo = split2(value)
            kc[sl, cols] = hi
            kc[sl, low] = lo
            return carry

        lax.fori_loop(0, NX, one, 0)

    def split_field(k, block):
        hi, lo = split2(block)
        vb[:, k * COLS : (k + 1) * COLS] = hi
        vb[:, (NZ + k) * COLS : (NZ + k + 1) * COLS] = lo

    def timed(c):
        sl = slice(c * ROWS // 2, (c + 1) * ROWS // 2)
        half = NZ * COLS
        acc = nt_dot(vb[sl, :half], tn[...]) + nt_dot(vb[sl, half:], tn[...])
        return acc[:, :COLS] + acc[:, COLS:]

    def split_w(it, c, k):
        hi, lo = split2(wy[it, c, k])
        j = c * NY + k
        wb[j * ROWS : (j + 1) * ROWS, :COLS] = hi
        wb[j * ROWS : (j + 1) * ROWS, COLS:] = lo

    def apply_rows(it, k):
        half = 8 * ROWS
        sl = slice(k * ROWS, (k + 1) * ROWS)
        acc = jnp.dot(kc[sl, :half], wb[...], preferred_element_type=F32)
        acc += jnp.dot(kc[sl, half:], wb[...], preferred_element_type=F32)
        p[it, k] = acc[:, :COLS] + acc[:, COLS:]

    HR = ROWS // 2
    A, B = pl.ds(0, HR), pl.ds(HR, HR)

    def spread(it):
        relay_r = copy(p.at[it, 2, A], rel.at[it, 0], right)
        relay_l = copy(p.at[it, 2, B], rel.at[it, 1], left)
        own_r = copy(p.at[it, 3, B], fin.at[it, 0, B], right)
        own_l = copy(p.at[it, 1, A], fin.at[it, 1, A], left)
        sum_r = copy(p.at[it, 3, A], fin.at[it, 0, A], right)
        sum_l = copy(p.at[it, 1, B], fin.at[it, 1, B], left)
        apply_rows(it, 2)
        relay_r.start()
        relay_l.start()
        apply_rows(it, 3)
        own_r.start()
        apply_rows(it, 1)
        own_l.start()
        relay_r.wait_recv()
        p[it, 3, A] += rel[it, 0]
        sum_r.start()
        relay_l.wait_recv()
        p[it, 1, B] += rel[it, 1]
        sum_l.start()
        apply_rows(it, 0)
        own_r.wait_recv()
        own_l.wait_recv()
        sum_r.wait_recv()
        sum_l.wait_recv()
        return p[it, 0] + fin[it, 0] + fin[it, 1]

    split_field(0, zg[0, 0])
    ring_step1(dfx, 2, False)
    ring_step1(dfy, 2, True)
    build_left(0)
    z_step(dz, 1)
    ring_step2(dfx, 2, False)
    ring_step2(dfy, 2, True)
    for k in (1, 3, 2):
        build_left(k)
    split_field(1, zg[0, 1])
    split_field(7, zg[0, 7])
    make_kernel(0, 0)
    make_kernel(0, 1)
    z_step(dz, 2)
    split_field(2, zg[0, 2])
    split_field(6, zg[0, 6])
    make_kernel(0, 3)
    make_kernel(0, 2)
    z_step(dz, 3)
    split_field(3, zg[0, 3])
    split_field(5, zg[0, 5])
    mate_wait(dfy, 2, 0)
    make_kernel(1, 0)
    mate_wait(dfy, 2, 1)
    make_kernel(1, 1)
    z_step(dz, 4)
    split_field(4, zg[0, 4])

    def send_w(it):
        d = y_ring(lambda c, k, h: wy.at[it, c, k, pl.ds(h * HR, HR)], 2)
        for h in range(2):
            wy[it, 0, 0, h * HR : (h + 1) * HR] = timed(h)
            d["R1", h].start()
            d["L1", h].start()
            d["m", 0, h].start()
        return d

    dw = send_w(0)
    mate_wait(dfy, 2, 3)
    make_kernel(1, 3)
    ring_step1(dw, 2, True)
    mate_wait(dfy, 2, 2)
    make_kernel(1, 2)

    def finish_w(it, d, stepped):
        split_w(it, 0, 0)
        if not stepped:
            ring_step1(d, 2, True)
        split_w(it, 0, 1)
        split_w(it, 0, 3)
        mate_wait(d, 2, 0)
        split_w(it, 1, 0)
        ring_step2(d, 2, True)
        split_w(it, 0, 2)
        for k in (1, 3, 2):
            mate_wait(d, 2, k)
            split_w(it, 1, k)

    finish_w(0, dw, True)
    total = spread(0)
    r0 = zg[0, 0]
    q = mk[...] * total + nz[...] * r0
    zg[1, 0] = q

    dz = z_ring(1)
    for c in range(CHUNKS):
        z_start(dz, c)
    sum_start(0, r0 * r0, r0 * q)
    z_step(dz, 1)
    sum_middle(0)
    z_step(dz, 2)
    norm0, curv0 = sum_end(0)
    alpha = norm0 / curv0

    def residual_block(k):
        return zg[0, k] - alpha * zg[1, k]

    r1 = residual_block(0)
    res[...] = r1
    sum_start(1, r1 * r1, r1)
    split_field(0, r1)
    for k in (1, 7, 2, 6):
        split_field(k, residual_block(k))
    z_step(dz, 3)
    for k in (3, 5):
        split_field(k, residual_block(k))
    sum_middle(1)
    z_step(dz, 4)
    split_field(4, residual_block(4))
    dw = send_w(1)
    norm1, _ = sum_end(1)
    finish_w(1, dw, False)
    total = spread(1)

    beta = norm1 / norm0
    r1 = res[...]
    d1 = r1 + beta * zg[0, 0]
    image = mk[...] * total + nz[...] * r1 + beta * zg[1, 0]
    sum_start(2, d1 * image, d1)
    p[1, 0] = d1
    p[0, 0] = image
    sum_middle(2)
    curv1, _ = sum_end(2)
    alpha1 = norm1 / curv1
    sol[...] = alpha * zg[0, 0] + alpha1 * p[1, 0]
    res[...] = res[...] - alpha1 * p[0, 0]

    for d in copies:
        d.wait_send()
    for n in range(3):
        whole(n, 0).wait_send()
        whole(n, 1).wait_send()


def body(targets, features, inv_scales, noise, time_kernel, block_mask):
    vmem = pl.BlockSpec(memory_space=pltpu.VMEM)
    block = jax.ShapeDtypeStruct((ROWS, COLS), F32)
    return pl.pallas_call(
        kernel,
        out_shape=(block, block),
        in_specs=[vmem] * 6,
        out_specs=(vmem, vmem),
        scratch_shapes=[
            pltpu.VMEM((2, NZ, ROWS, COLS), F32),
            pltpu.VMEM((2, NCORE, NY, ROWS, COLS), F32),
            pltpu.VMEM((NCORE, NY, FEAT, ROWS), F32),
            pltpu.VMEM((NX, FEAT, ROWS), F32),
            pltpu.VMEM((NX * ROWS, DEPTH), BF16),
            pltpu.VMEM((DEPTH, 8 * ROWS), BF16),
            pltpu.VMEM((NX * ROWS, 16 * ROWS), BF16),
            pltpu.VMEM((8 * ROWS, 2 * COLS), BF16),
            pltpu.VMEM((ROWS, 2 * NZ * COLS), BF16),
            pltpu.VMEM((2 * COLS, NZ * COLS), BF16),
            pltpu.VMEM((2, NX, ROWS, COLS), F32),
            pltpu.VMEM((2, 2, ROWS // 2, COLS), F32),
            pltpu.VMEM((2, 2, ROWS, COLS), F32),
            pltpu.VMEM((ROWS, COLS), F32),
            pltpu.VMEM((ROWS, COLS), F32),
            pltpu.VMEM((3, 2, 2, COLS), F32),
            pltpu.VMEM((3, PLANE - 1, 2, COLS), F32),
            pltpu.VMEM((3, NZ - 1, 2, COLS), F32),
            pltpu.SemaphoreType.DMA((NSEM,)),
            pltpu.SemaphoreType.DMA((NSEM,)),
            pltpu.SemaphoreType.DMA((3, 2)),
            pltpu.SemaphoreType.DMA((3, 2)),
        ],
        compiler_params=pltpu.CompilerParams(
            collective_id=0, has_side_effects=True, vmem_limit_bytes=40 * 1024 * 1024
        ),
    )(
        targets, features.T, inv_scales.reshape(1, FEAT), noise.reshape(1, ROWS), time_kernel, block_mask.T
    )


def solution(mesh):
    return jax.shard_map(
        body,
        mesh=mesh,
        in_specs=(P("cfg", "tm"), P("cfg", None), P(), P("cfg"), P("tm", None), P("cfg", "tm")),
        out_specs=(P("cfg", "tm"), P("cfg", "tm")),
        check_vma=False,
    )
```

```python
import math

import jax
import jax.numpy as jnp
from jax import lax
from jax.experimental import pallas as pl
from jax.experimental.pallas import tpu as pltpu
from jax.sharding import PartitionSpec as P

MESH = pl.DeviceIdType.MESH
F32, BF16 = jnp.float32, jnp.bfloat16
NY, NX, NCORE, NZ = 4, 4, 2, 8
PLANE = NY * NX * NCORE
ROWS, COLS, FEAT = 256, 128, 64
DEPTH = 384
CHUNKS = 4
NSEM = 256
UNIT = math.sqrt(3.0) * math.log2(math.e)
LN2 = math.log(2.0)
PLACE = (0, 1, 3, 2)


def split2(x):
    hi = x.astype(BF16)
    return hi, (x - hi.astype(F32)).astype(BF16)


def nt_dot(a, b):
    return lax.dot_general(a, b, (((1,), (1,)), ((), ())), preferred_element_type=F32)


def kernel(
    tgt_hbm, feat_hbm, isc_hbm, noise_hbm, tk_hbm, bm_hbm, sol, res,
    tgt, feat, isc, noise_ref, tk, bm, ins,
    zg, gx, wy, fy, fx, fl, fr, kc, wb, vb, tn, p, rel, fin, nz, mk,
    arsrc, arp, arz, ss, rs, ars, arr,
):
    me, z = lax.axis_index("cfg"), lax.axis_index("tm")
    core = lax.rem(me, NCORE)
    x = lax.rem(me // NCORE, NX)
    y = me // (NCORE * NX)

    def at(yy, xx, cc):
        return ((yy * NX + xx) * NCORE + cc, z)

    right, left = at(y, lax.rem(x + 1, NX), core), at(y, lax.rem(x + NX - 1, NX), core)
    up, down = at(lax.rem(y + 1, NY), x, core), at(lax.rem(y + NY - 1, NY), x, core)
    mate = at(y, x, 1 - core)
    zup, zdown = (me, lax.rem(z + 1, NZ)), (me, lax.rem(z + NZ - 1, NZ))
    plane = [(lax.rem(me + r, PLANE), z) for r in range(1, PLANE)]
    column = [(me, lax.rem(z + r, NZ)) for r in range(1, NZ)]

    copies = []

    def copy(src, dst, dev):
        i = len(copies)
        assert i < NSEM
        d = pltpu.make_async_remote_copy(
            src_ref=src, dst_ref=dst, send_sem=ss.at[i], recv_sem=rs.at[i],
            device_id=dev, device_id_type=MESH,
        )
        copies.append(d)
        return d

    pairs = ((bm_hbm, bm), (tgt_hbm, tgt), (isc_hbm, isc), (feat_hbm, feat), (noise_hbm, noise_ref), (tk_hbm, tk))
    loads = [pltpu.make_async_copy(a, b, ins.at[i]) for i, (a, b) in enumerate(pairs)]
    for d in loads:
        d.start()
    barrier = pltpu.get_barrier_semaphore()
    near = [mate, right, left, up, down, zup, zdown]
    for dev in near:
        pl.semaphore_signal(barrier, inc=1, device_id=dev, device_id_type=MESH)

    for d in loads[:4]:
        d.wait()
    mk[...] = jnp.broadcast_to(bm[...].astype(F32), (COLS, ROWS)).T
    r0 = mk[...] * tgt[...]
    zg[0, 0] = r0
    gx[0, 0] = r0
    fscaled = feat[...] * (isc[...].T * UNIT)
    fy[0, 0] = fscaled
    fx[0] = fscaled

    pl.semaphore_wait(barrier, len(near))

    def ring4(buf, nh, fwd, back):
        d = {}
        for h in range(nh):
            d["R1", h] = copy(buf(0, h), buf(1, h), fwd)
            d["L1", h] = copy(buf(0, h), buf(3, h), back)
        for h in range(nh):
            if h < nh // 2:
                d["2", h] = copy(buf(1, h), buf(2, h), fwd)
            else:
                d["2", h] = copy(buf(3, h), buf(2, h), back)
        return d

    def y_ring(buf, nh):
        d = ring4(lambda k, h: buf(0, k, h), nh, up, down)
        for k in (0, 1, 3, 2):
            for h in range(nh):
                d["m", k, h] = copy(buf(0, k, h), buf(1, k, h), mate)
        return d

    def order(nh):
        return [(h, (h + nh // 2) % nh) for h in range(nh)]

    def ring_start(d, nh):
        for h, g in order(nh):
            d["R1", h].start()
            d["L1", g].start()

    def ring_step1(d, nh, mated):
        for h, g in order(nh):
            d["R1", h].wait_recv()
            if h < nh // 2:
                d["2", h].start()
            d["L1", g].wait_recv()
            if g >= nh // 2:
                d["2", g].start()
            if mated:
                d["m", 1, h].start()
                d["m", 3, g].start()

    def ring_step2(d, nh, mated):
        for h, g in order(nh)[: nh // 2]:
            for e in (h, g):
                d["2", e].wait_recv()
                if mated:
                    d["m", 2, e].start()

    def mate_wait(d, nh, k):
        for h in range(nh):
            d["m", k, h].wait_recv()

    CR = ROWS // CHUNKS

    def z_ring(it):
        d = {}
        for s in range(1, 5):
            for c in range(CHUNKS):
                sl = pl.ds(c * CR, CR)
                if s < 4 or c < CHUNKS // 2:
                    d["R", s, c] = copy(zg.at[it, s - 1, sl], zg.at[it, s, sl], zup)
                if s < 4 or c >= CHUNKS // 2:
                    d["L", s, c] = copy(zg.at[it, (9 - s) % 8, sl], zg.at[it, 8 - s, sl], zdown)
        return d

    def z_start(d, c):
        d["R", 1, c].start()
        d["L", 1, (c + CHUNKS // 2) % CHUNKS].start()

    def z_events(d):
        for s in range(1, 5):
            for c in range(CHUNKS if s < 4 else CHUNKS // 2):
                for way, e in (("R", c), ("L", (c + CHUNKS // 2) % CHUNKS)):
                    d[way, s, e].wait_recv()
                    if (way, s + 1, e) in d:
                        d[way, s + 1, e].start()
                yield

    def pump(events, n):
        for _ in range(n):
            next(events)

    def plane_copies(n):
        return [
            pltpu.make_async_remote_copy(
                src_ref=arsrc.at[n, 0], dst_ref=arp.at[n, r], send_sem=ars.at[n, 0], recv_sem=arr.at[n, 0],
                device_id=dev, device_id_type=MESH,
            )
            for r, dev in enumerate(plane)
        ]

    def column_copies(n):
        return [
            pltpu.make_async_remote_copy(
                src_ref=arsrc.at[n, 1], dst_ref=arz.at[n, r], send_sem=ars.at[n, 1], recv_sem=arr.at[n, 1],
                device_id=dev, device_id_type=MESH,
            )
            for r, dev in enumerate(column)
        ]

    def whole(n, j):
        buf, dev = (arp, plane[0]) if j == 0 else (arz, column[0])
        return pltpu.make_async_remote_copy(
            src_ref=buf.at[n], dst_ref=buf.at[n], send_sem=ars.at[n, j], recv_sem=arr.at[n, j],
            device_id=dev, device_id_type=MESH,
        )

    def sum_start(n, first, second):
        arsrc[n, 0, 0:1] = jnp.sum(first, axis=0, keepdims=True)
        arsrc[n, 0, 1:2] = jnp.sum(second, axis=0, keepdims=True)
        for d in plane_copies(n):
            d.start()

    def sum_middle(n):
        whole(n, 0).wait_recv()
        arsrc[n, 1] = arsrc[n, 0] + jnp.sum(arp[n], axis=0)
        for d in column_copies(n):
            d.start()

    def sum_end(n):
        whole(n, 1).wait_recv()
        both = arsrc[n, 1] + jnp.sum(arz[n], axis=0)
        both = jnp.sum(both, axis=1, keepdims=True)
        return both[0:1], both[1:2]

    dz = z_ring(0)
    for c in range(CHUNKS):
        z_start(dz, c)
    FH = ROWS // 2
    dfx = ring4(lambda k, h: fx.at[k, :, pl.ds(h * FH, FH)], 2, right, left)
    dfy = y_ring(lambda c, k, h: fy.at[c, k, :, pl.ds(h * FH, FH)], 2)
    ring_start(dfy, 2)
    ring_start(dfx, 2)
    for h in range(2):
        dfy["m", 0, h].start()

    loads[4].wait()
    nz[...] = jnp.broadcast_to(noise_ref[...], (COLS, ROWS)).T
    loads[5].wait()
    for k in range(NZ):
        o = lax.rem(z + NZ - k, NZ)
        hi, lo = split2(tk[:, pl.ds(pl.multiple_of(o * COLS, COLS), COLS)])
        tn[0:COLS, k * COLS : (k + 1) * COLS] = hi
        tn[COLS : 2 * COLS, k * COLS : (k + 1) * COLS] = lo

    def parts(block):
        hi = block.astype(BF16).astype(F32)
        lo = (block - hi).astype(BF16).astype(F32)
        kept = hi + lo
        n = jnp.sum(kept * kept, axis=0, keepdims=True)
        n1 = n.astype(BF16).astype(F32)
        n2 = (n - n1).astype(BF16).astype(F32)
        return hi, lo, jnp.concatenate([n1, n2, n - n1 - n2], axis=0)

    pad = DEPTH - 4 * FEAT
    row = lax.broadcasted_iota(jnp.int32, (pad, ROWS), 0)

    def place(n, first):
        out = jnp.where((row >= 3 - first) & (row < 6 - first), 1.0, 0.0)
        for i in range(3):
            out = jnp.where(row == first + i, jnp.broadcast_to(n[i : i + 1], (pad, ROWS)), out)
        return out

    def build_left(k):
        hi, lo, n = parts(fx[k])
        stack = jnp.concatenate([-2.0 * hi, -2.0 * hi, -2.0 * lo, -2.0 * lo, place(n, 0)], axis=0)
        i = PLACE[k]
        fl[i * ROWS : (i + 1) * ROWS, :] = stack.T.astype(BF16)

    def build_right(c, k):
        hi, lo, n = parts(fy[c, k])
        stack = jnp.concatenate([hi, lo, hi, lo, place(n, 3)], axis=0)
        j = c * NY + k
        fr[:, j * ROWS : (j + 1) * ROWS] = stack.astype(BF16)

    def make_kernel(c, k, first, end):
        j = c * NY + k
        cols = slice(j * ROWS, (j + 1) * ROWS)
        low = slice((8 + j) * ROWS, (9 + j) * ROWS)

        def one(i, carry):
            sl = pl.ds(pl.multiple_of(i * ROWS, ROWS), ROWS)
            d2 = jnp.dot(fl[sl, :], fr[:, cols], preferred_element_type=F32)
            d2 = jnp.maximum(d2, 1e-30)
            u = d2 * lax.rsqrt(d2)
            value = (1.0 + LN2 * u) * jnp.exp2(-u)
            hi, lo = split2(value)
            kc[sl, cols] = hi
            kc[sl, low] = lo
            return carry

        lax.fori_loop(first, end, one, 0)

    def split_field(k, block):
        hi, lo = split2(block)
        vb[:, k * COLS : (k + 1) * COLS] = hi
        vb[:, (NZ + k) * COLS : (NZ + k + 1) * COLS] = lo

    def timed(c):
        sl = slice(c * ROWS // 2, (c + 1) * ROWS // 2)
        half = NZ * COLS
        acc = nt_dot(vb[sl, :half], tn[...]) + nt_dot(vb[sl, half:], tn[...])
        return acc[:, :COLS] + acc[:, COLS:]

    def split_w(it, c, k):
        hi, lo = split2(wy[it, c, k])
        j = c * NY + k
        wb[j * ROWS : (j + 1) * ROWS, :COLS] = hi
        wb[j * ROWS : (j + 1) * ROWS, COLS:] = lo

    def apply_rows(it, k, early):
        n = ROWS
        sl = slice(PLACE[k] * n, (PLACE[k] + 1) * n)
        acc = None
        for lo, hi in ((0, 2), (3, 6), (7, 8)) if early else ((2, 3), (6, 7)):
            for off in (0, 8):
                part = jnp.dot(kc[sl, (off + lo) * n : (off + hi) * n], wb[lo * n : hi * n, :], preferred_element_type=F32)
                acc = part if acc is None else acc + part
        out = acc[:, :COLS] + acc[:, COLS:]
        if early:
            p[it, k] = out
        else:
            p[it, k] += out

    HR = ROWS // 2
    A, B = pl.ds(0, HR), pl.ds(HR, HR)

    def spread(it, last):
        half = CHUNKS // 2
        sl = [pl.ds(c * CR, CR) for c in range(CHUNKS)]
        d = {}
        for c in range(CHUNKS):
            if c < half:
                d["relay", c] = copy(p.at[it, 2, sl[c]], rel.at[it, 0, sl[c]], right)
                d["own", c] = copy(p.at[it, 1, sl[c]], fin.at[it, 1, sl[c]], left)
                d["sum", c] = copy(p.at[it, 3, sl[c]], fin.at[it, 0, sl[c]], right)
            else:
                d["relay", c] = copy(p.at[it, 2, sl[c]], rel.at[it, 0, sl[c]], left)
                d["own", c] = copy(p.at[it, 3, sl[c]], fin.at[it, 0, sl[c]], right)
                d["sum", c] = copy(p.at[it, 1, sl[c]], fin.at[it, 1, sl[c]], left)
        turns = [e for c in range(half) for e in (c, c + half)]
        apply_rows(it, 2, False)
        if last is not None:
            apply_rows(it, 3, False)
            apply_rows(it, 1, False)
            apply_rows(it, 0, False)
            last()
        for c in turns:
            d["relay", c].start()
        if last is None:
            apply_rows(it, 3, False)
            apply_rows(it, 1, False)
        for c in turns:
            d["own", c].start()
        if last is None:
            apply_rows(it, 0, False)
        for c in turns:
            d["relay", c].wait_recv()
            k = 3 if c < half else 1
            p[it, k, sl[c]] += rel[it, 0, sl[c]]
            d["sum", c].start()
        for c in turns:
            d["own", c].wait_recv()
            d["sum", c].wait_recv()
            yield sl[c], p[it, 0, sl[c]] + fin[it, 0, sl[c]] + fin[it, 1, sl[c]]

    def x_ring(i):
        return ring4(lambda k, h: gx.at[i, k, pl.ds(h * HR, HR)], 2, right, left)

    def send_w(it):
        d = y_ring(lambda c, k, h: wy.at[it, c, k, pl.ds(h * CR, CR)], CHUNKS)
        for h in range(2):
            wy[it, 0, 0, h * HR : (h + 1) * HR] = timed(h)
        ring_start(d, CHUNKS)
        for h in range(CHUNKS):
            d["m", 0, h].start()
        return d


    def finish_w(it, d, stepped):
        split_w(it, 0, 0)
        mate_wait(d, CHUNKS, 0)
        split_w(it, 1, 0)
        if not stepped:
            ring_step1(d, CHUNKS, True)
        split_w(it, 0, 1)
        split_w(it, 0, 3)
        for k in (1, 3):
            mate_wait(d, CHUNKS, k)
            split_w(it, 1, k)
        for k in (2, 3, 1, 0):
            apply_rows(it, k, True)
        ring_step2(d, CHUNKS, True)
        split_w(it, 0, 2)
        mate_wait(d, CHUNKS, 2)
        split_w(it, 1, 2)

    ev = z_events(dz)
    split_field(0, zg[0, 0])
    build_left(0)
    build_right(0, 0)
    ring_step1(dfx, 2, False)
    ring_step1(dfy, 2, True)
    pump(ev, 1)
    build_left(1)
    build_left(3)
    make_kernel(0, 0, 0, 3)
    pump(ev, 1)
    mate_wait(dfy, 2, 0)
    build_right(1, 0)
    make_kernel(1, 0, 0, 3)
    pump(ev, 1)
    build_right(0, 1)
    make_kernel(0, 1, 0, 3)
    pump(ev, 1)
    ring_step2(dfx, 2, False)
    ring_step2(dfy, 2, True)
    dx = x_ring(0)
    ring_start(dx, 2)
    build_left(2)
    split_field(1, zg[0, 1])
    split_field(7, zg[0, 7])
    build_right(0, 3)
    make_kernel(0, 3, 0, 4)
    pump(ev, 1)
    make_kernel(0, 0, 3, 4)
    make_kernel(1, 0, 3, 4)
    make_kernel(0, 1, 3, 4)
    pump(ev, 1)
    build_right(0, 2)
    make_kernel(0, 2, 0, 4)
    pump(ev, 2)
    split_field(2, zg[0, 2])
    split_field(6, zg[0, 6])
    mate_wait(dfy, 2, 1)
    build_right(1, 1)
    make_kernel(1, 1, 0, 4)
    pump(ev, 1)
    ring_step1(dx, 2, False)
    mate_wait(dfy, 2, 3)
    build_right(1, 3)
    make_kernel(1, 3, 0, 4)
    pump(ev, 1)
    mate_wait(dfy, 2, 2)
    build_right(1, 2)
    make_kernel(1, 2, 0, 4)
    pump(ev, 2)
    ring_step2(dx, 2, False)
    split_field(3, zg[0, 3])
    split_field(5, zg[0, 5])
    pump(ev, 2)
    split_field(4, zg[0, 4])
    dw = send_w(0)
    finish_w(0, dw, False)

    dz = z_ring(1)
    for i, (sl, total) in enumerate(spread(0, None)):
        q = mk[sl, :] * total + nz[sl, :] * gx[0, 0, sl]
        zg[1, 0, sl] = q
        gx[1, 0, sl] = q
        c = (i % 2) * CHUNKS // 2 + i // 2
        for way in "RL" if i % 2 == 0 else "LR":
            dz[way, 1, c].start()
    r0, q = zg[0, 0], zg[1, 0]
    sum_start(0, r0 * r0, r0 * q)
    dx = x_ring(1)
    ring_start(dx, 2)
    ev = z_events(dz)
    pump(ev, 3)
    sum_middle(0)
    pump(ev, 5)
    norm0, curv0 = sum_end(0)
    alpha = norm0 / curv0

    def residual_block(k):
        return zg[0, k] - alpha * zg[1, k]

    r1 = residual_block(0)
    sum_start(1, r1 * r1, r1)
    ring_step1(dx, 2, False)
    split_field(0, r1)
    for k in (1, 7, 2, 6):
        split_field(k, residual_block(k))
    pump(ev, 4)
    for k in (3, 5):
        split_field(k, residual_block(k))
    pump(ev, 2)
    split_field(4, residual_block(4))
    dw = send_w(1)
    sum_middle(1)
    ring_step2(dx, 2, False)
    finish_w(1, dw, False)
    norm1, _ = sum_end(1)
    beta = norm1 / norm0

    def curvature():
        r1 = gx[0, 0] - alpha * gx[1, 0]
        d1 = r1 + beta * gx[0, 0]
        terms = d1 * (p[1, 0] + nz[...] * r1 + beta * gx[1, 0])
        for k in (1, 2, 3):
            terms += p[1, k] * (gx[0, k] - alpha * gx[1, k] + beta * gx[0, k])
        sum_start(2, terms, terms)

    for i, (sl, total) in enumerate(spread(1, curvature)):
        if i == 0:
            sum_middle(2)
        r1 = gx[0, 0, sl] - alpha * gx[1, 0, sl]
        res[sl, :] = mk[sl, :] * total + nz[sl, :] * r1 + beta * gx[1, 0, sl]
    curv1, _ = sum_end(2)
    alpha1 = norm1 / curv1
    r0 = gx[0, 0]
    r1 = r0 - alpha * gx[1, 0]
    sol[...] = alpha * r0 + alpha1 * (r1 + beta * r0)
    res[...] = r1 - alpha1 * res[...]

    for d in copies:
        d.wait_send()
    for n in range(3):
        whole(n, 0).wait_send()
        whole(n, 1).wait_send()


def body(targets, features, inv_scales, noise, time_kernel, block_mask):
    vmem = pl.BlockSpec(memory_space=pltpu.VMEM)
    block = jax.ShapeDtypeStruct((ROWS, COLS), F32)
    return pl.pallas_call(
        kernel,
        out_shape=(block, block),
        in_specs=[pl.BlockSpec(memory_space=pl.ANY)] * 6,
        out_specs=(vmem, vmem),
        scratch_shapes=[
            pltpu.VMEM((ROWS, COLS), F32),
            pltpu.VMEM((FEAT, ROWS), F32),
            pltpu.VMEM((1, FEAT), F32),
            pltpu.VMEM((1, ROWS), F32),
            pltpu.VMEM((COLS, NZ * COLS), F32),
            pltpu.VMEM((1, ROWS), jnp.int32),
            pltpu.SemaphoreType.DMA((6,)),
            pltpu.VMEM((2, NZ, ROWS, COLS), F32),
            pltpu.VMEM((2, NX, ROWS, COLS), F32),
            pltpu.VMEM((2, NCORE, NY, ROWS, COLS), F32),
            pltpu.VMEM((NCORE, NY, FEAT, ROWS), F32),
            pltpu.VMEM((NX, FEAT, ROWS), F32),
            pltpu.VMEM((NX * ROWS, DEPTH), BF16),
            pltpu.VMEM((DEPTH, 8 * ROWS), BF16),
            pltpu.VMEM((NX * ROWS, 16 * ROWS), BF16),
            pltpu.VMEM((8 * ROWS, 2 * COLS), BF16),
            pltpu.VMEM((ROWS, 2 * NZ * COLS), BF16),
            pltpu.VMEM((2 * COLS, NZ * COLS), BF16),
            pltpu.VMEM((2, NX, ROWS, COLS), F32),
            pltpu.VMEM((2, 1, ROWS, COLS), F32),
            pltpu.VMEM((2, 2, ROWS, COLS), F32),
            pltpu.VMEM((ROWS, COLS), F32),
            pltpu.VMEM((ROWS, COLS), F32),
            pltpu.VMEM((3, 2, 2, COLS), F32),
            pltpu.VMEM((3, PLANE - 1, 2, COLS), F32),
            pltpu.VMEM((3, NZ - 1, 2, COLS), F32),
            pltpu.SemaphoreType.DMA((NSEM,)),
            pltpu.SemaphoreType.DMA((NSEM,)),
            pltpu.SemaphoreType.DMA((3, 2)),
            pltpu.SemaphoreType.DMA((3, 2)),
        ],
        compiler_params=pltpu.CompilerParams(
            collective_id=0, has_side_effects=True, vmem_limit_bytes=67043328
        ),
    )(
        targets, features.T, inv_scales.reshape(1, FEAT), noise.reshape(1, ROWS), time_kernel, block_mask.T
    )


def solution(mesh):
    return jax.shard_map(
        body,
        mesh=mesh,
        in_specs=(P("cfg", "tm"), P("cfg", None), P(), P("cfg"), P("tm", None), P("cfg", "tm")),
        out_specs=(P("cfg", "tm"), P("cfg", "tm")),
        check_vma=False,
    )
```

```python
import math

import jax
import jax.numpy as jnp
from jax import lax
from jax.experimental import pallas as pl
from jax.experimental.pallas import tpu as pltpu
from jax.sharding import PartitionSpec as P

MESH = pl.DeviceIdType.MESH
F32, BF16 = jnp.float32, jnp.bfloat16
NY, NX, NCORE, NZ = 4, 4, 2, 8
PLANE = NY * NX * NCORE
ROWS, COLS, FEAT = 256, 128, 64
DEPTH = 384
CHUNKS = 4
NSEM = 256
UNIT = math.sqrt(3.0) * math.log2(math.e)
LN2 = math.log(2.0)
PLACE = (0, 1, 3, 2)


def split2(x):
    hi = x.astype(BF16)
    return hi, (x - hi.astype(F32)).astype(BF16)


def nt_dot(a, b):
    return lax.dot_general(a, b, (((1,), (1,)), ((), ())), preferred_element_type=F32)


def kernel(
    tgt_hbm, feat_hbm, isc_hbm, noise_hbm, tk_hbm, bm_hbm, sol, res,
    tgt, feat, isc, noise_ref, tk, bm, ins,
    zg, gx, wy, fy, fx, fl, fr, kc, wb, vb, tn, p, rel, fin, nz, mk,
    arsrc, arp, arz, ss, rs, ars, arr,
):
    me, z = lax.axis_index("cfg"), lax.axis_index("tm")
    core = lax.rem(me, NCORE)
    x = lax.rem(me // NCORE, NX)
    y = me // (NCORE * NX)

    def at(yy, xx, cc):
        return ((yy * NX + xx) * NCORE + cc, z)

    right, left = at(y, lax.rem(x + 1, NX), core), at(y, lax.rem(x + NX - 1, NX), core)
    up, down = at(lax.rem(y + 1, NY), x, core), at(lax.rem(y + NY - 1, NY), x, core)
    mate = at(y, x, 1 - core)
    zup, zdown = (me, lax.rem(z + 1, NZ)), (me, lax.rem(z + NZ - 1, NZ))
    plane = [(lax.rem(me + r, PLANE), z) for r in range(1, PLANE)]
    column = [(me, lax.rem(z + r, NZ)) for r in range(1, NZ)]

    copies = []

    def copy(src, dst, dev):
        i = len(copies)
        assert i < NSEM
        d = pltpu.make_async_remote_copy(
            src_ref=src, dst_ref=dst, send_sem=ss.at[i], recv_sem=rs.at[i],
            device_id=dev, device_id_type=MESH,
        )
        copies.append(d)
        return d

    pairs = ((bm_hbm, bm), (tgt_hbm, tgt), (isc_hbm, isc), (feat_hbm, feat), (noise_hbm, noise_ref), (tk_hbm, tk))
    loads = [pltpu.make_async_copy(a, b, ins.at[i]) for i, (a, b) in enumerate(pairs)]
    for d in loads:
        d.start()
    barrier = pltpu.get_barrier_semaphore()
    near = [mate, right, left, up, down, zup, zdown]
    for dev in near:
        pl.semaphore_signal(barrier, inc=1, device_id=dev, device_id_type=MESH)

    for d in loads[:4]:
        d.wait()
    mk[...] = jnp.broadcast_to(bm[...].astype(F32), (COLS, ROWS)).T
    r0 = mk[...] * tgt[...]
    zg[0, 0] = r0
    gx[0, 0] = r0
    fscaled = feat[...] * (isc[...].T * UNIT)
    fy[0, 0] = fscaled
    fx[0] = fscaled

    pl.semaphore_wait(barrier, len(near))

    def ring4(buf, nh, fwd, back):
        d = {}
        for h in range(nh):
            d["R1", h] = copy(buf(0, h), buf(1, h), fwd)
            d["L1", h] = copy(buf(0, h), buf(3, h), back)
        for h in range(nh):
            if h < nh // 2:
                d["2", h] = copy(buf(1, h), buf(2, h), fwd)
            else:
                d["2", h] = copy(buf(3, h), buf(2, h), back)
        return d

    def y_ring(buf, nh):
        d = ring4(lambda k, h: buf(0, k, h), nh, up, down)
        for k in (0, 1, 3, 2):
            for h in range(nh):
                d["m", k, h] = copy(buf(0, k, h), buf(1, k, h), mate)
        return d

    def order(nh):
        return [(h, (h + nh // 2) % nh) for h in range(nh)]

    def ring_start(d, nh):
        for h, g in order(nh):
            d["R1", h].start()
            d["L1", g].start()

    def ring_step1(d, nh, mated):
        for h, g in order(nh):
            d["R1", h].wait_recv()
            if h < nh // 2:
                d["2", h].start()
            d["L1", g].wait_recv()
            if g >= nh // 2:
                d["2", g].start()
            if mated:
                d["m", 1, h].start()
                d["m", 3, g].start()

    def ring_step2(d, nh, mated):
        for h, g in order(nh)[: nh // 2]:
            for e in (h, g):
                d["2", e].wait_recv()
                if mated:
                    d["m", 2, e].start()

    def mate_wait(d, nh, k):
        for h in range(nh):
            d["m", k, h].wait_recv()

    CR = ROWS // CHUNKS

    def z_ring(it):
        d = {}
        for s in range(1, 5):
            for c in range(CHUNKS):
                sl = pl.ds(c * CR, CR)
                if s < 4 or c < CHUNKS // 2:
                    d["R", s, c] = copy(zg.at[it, s - 1, sl], zg.at[it, s, sl], zup)
                if s < 4 or c >= CHUNKS // 2:
                    d["L", s, c] = copy(zg.at[it, (9 - s) % 8, sl], zg.at[it, 8 - s, sl], zdown)
        return d

    def z_start(d, c):
        d["R", 1, c].start()
        d["L", 1, (c + CHUNKS // 2) % CHUNKS].start()

    def z_events(d):
        for s in range(1, 5):
            for c in range(CHUNKS if s < 4 else CHUNKS // 2):
                for way, e in (("R", c), ("L", (c + CHUNKS // 2) % CHUNKS)):
                    d[way, s, e].wait_recv()
                    if (way, s + 1, e) in d:
                        d[way, s + 1, e].start()
                yield

    def pump(events, n):
        for _ in range(n):
            next(events)

    def plane_copies(n):
        return [
            pltpu.make_async_remote_copy(
                src_ref=arsrc.at[n, 0], dst_ref=arp.at[n, r], send_sem=ars.at[n, 0], recv_sem=arr.at[n, 0],
                device_id=dev, device_id_type=MESH,
            )
            for r, dev in enumerate(plane)
        ]

    def column_copies(n):
        return [
            pltpu.make_async_remote_copy(
                src_ref=arsrc.at[n, 1], dst_ref=arz.at[n, r], send_sem=ars.at[n, 1], recv_sem=arr.at[n, 1],
                device_id=dev, device_id_type=MESH,
            )
            for r, dev in enumerate(column)
        ]

    def whole(n, j):
        buf, dev = (arp, plane[0]) if j == 0 else (arz, column[0])
        return pltpu.make_async_remote_copy(
            src_ref=buf.at[n], dst_ref=buf.at[n], send_sem=ars.at[n, j], recv_sem=arr.at[n, j],
            device_id=dev, device_id_type=MESH,
        )

    def sum_start(n, first, second):
        arsrc[n, 0, 0:1] = jnp.sum(first, axis=0, keepdims=True)
        arsrc[n, 0, 1:2] = jnp.sum(second, axis=0, keepdims=True)
        for d in plane_copies(n):
            d.start()

    def sum_middle(n):
        whole(n, 0).wait_recv()
        arsrc[n, 1] = arsrc[n, 0] + jnp.sum(arp[n], axis=0)
        for d in column_copies(n):
            d.start()

    def sum_end(n):
        whole(n, 1).wait_recv()
        both = arsrc[n, 1] + jnp.sum(arz[n], axis=0)
        both = jnp.sum(both, axis=1, keepdims=True)
        return both[0:1], both[1:2]

    dz = z_ring(0)
    for c in range(CHUNKS):
        z_start(dz, c)
    FH = ROWS // 2
    dfx = ring4(lambda k, h: fx.at[k, :, pl.ds(h * FH, FH)], 2, right, left)
    dfy = y_ring(lambda c, k, h: fy.at[c, k, :, pl.ds(h * FH, FH)], 2)
    ring_start(dfy, 2)
    ring_start(dfx, 2)
    for h in range(2):
        dfy["m", 0, h].start()

    loads[4].wait()
    nz[...] = jnp.broadcast_to(noise_ref[...], (COLS, ROWS)).T
    loads[5].wait()
    for k in range(NZ):
        o = lax.rem(z + NZ - k, NZ)
        hi, lo = split2(tk[:, pl.ds(pl.multiple_of(o * COLS, COLS), COLS)])
        tn[0:COLS, k * COLS : (k + 1) * COLS] = hi
        tn[COLS : 2 * COLS, k * COLS : (k + 1) * COLS] = lo

    def parts(block):
        hi = block.astype(BF16).astype(F32)
        lo = (block - hi).astype(BF16).astype(F32)
        kept = hi + lo
        n = jnp.sum(kept * kept, axis=0, keepdims=True)
        n1 = n.astype(BF16).astype(F32)
        n2 = (n - n1).astype(BF16).astype(F32)
        return hi, lo, jnp.concatenate([n1, n2, n - n1 - n2], axis=0)

    pad = DEPTH - 4 * FEAT
    row = lax.broadcasted_iota(jnp.int32, (pad, ROWS), 0)

    def place(n, first):
        out = jnp.where((row >= 3 - first) & (row < 6 - first), 1.0, 0.0)
        for i in range(3):
            out = jnp.where(row == first + i, jnp.broadcast_to(n[i : i + 1], (pad, ROWS)), out)
        return out

    def build_left(k):
        hi, lo, n = parts(fx[k])
        stack = jnp.concatenate([-2.0 * hi, -2.0 * hi, -2.0 * lo, -2.0 * lo, place(n, 0)], axis=0)
        i = PLACE[k]
        fl[i * ROWS : (i + 1) * ROWS, :] = stack.T.astype(BF16)

    def build_right(c, k):
        hi, lo, n = parts(fy[c, k])
        stack = jnp.concatenate([hi, lo, hi, lo, place(n, 3)], axis=0)
        j = c * NY + k
        fr[:, j * ROWS : (j + 1) * ROWS] = stack.astype(BF16)

    def make_kernel(c, k, first, end):
        j = c * NY + k
        cols = slice(j * ROWS, (j + 1) * ROWS)
        low = slice((8 + j) * ROWS, (9 + j) * ROWS)

        def one(i):
            sl = slice(i * ROWS, (i + 1) * ROWS)
            d2 = jnp.dot(fl[sl, :], fr[:, cols], preferred_element_type=F32)
            d2 = jnp.maximum(d2, 1e-30)
            u = d2 * lax.rsqrt(d2)
            value = (1.0 + LN2 * u) * jnp.exp2(-u)
            hi, lo = split2(value)
            kc[sl, cols] = hi
            kc[sl, low] = lo

        for i in range(first, end):
            one(i)

    def split_field(k, block):
        hi, lo = split2(block)
        vb[:, k * COLS : (k + 1) * COLS] = hi
        vb[:, (NZ + k) * COLS : (NZ + k + 1) * COLS] = lo

    def timed(spans):
        acc = None
        for off in (0, NZ):
            for lo, hi in spans:
                part = nt_dot(vb[:, (off + lo) * COLS : (off + hi) * COLS], tn[:, lo * COLS : hi * COLS])
                acc = part if acc is None else acc + part
        return acc[:, :COLS] + acc[:, COLS:]

    def timed_early(it):
        wy[it, 0, 0] = timed(((0, 4), (5, 8)))

    def split_w(it, c, k):
        hi, lo = split2(wy[it, c, k])
        j = c * NY + k
        wb[j * ROWS : (j + 1) * ROWS, :COLS] = hi
        wb[j * ROWS : (j + 1) * ROWS, COLS:] = lo

    def apply_rows(it, k, early):
        n = ROWS
        sl = slice(PLACE[k] * n, (PLACE[k] + 1) * n)
        acc = None
        for lo, hi in ((0, 2), (3, 6), (7, 8)) if early else ((2, 3), (6, 7)):
            for off in (0, 8):
                part = jnp.dot(kc[sl, (off + lo) * n : (off + hi) * n], wb[lo * n : hi * n, :], preferred_element_type=F32)
                acc = part if acc is None else acc + part
        out = acc[:, :COLS] + acc[:, COLS:]
        if early:
            p[it, k] = out
        else:
            p[it, k] += out

    HR = ROWS // 2
    A, B = pl.ds(0, HR), pl.ds(HR, HR)

    def spread(it, last):
        half = CHUNKS // 2
        sl = [pl.ds(c * CR, CR) for c in range(CHUNKS)]
        d = {}
        for c in range(CHUNKS):
            if c < half:
                d["relay", c] = copy(p.at[it, 2, sl[c]], rel.at[it, 0, sl[c]], right)
                d["own", c] = copy(p.at[it, 1, sl[c]], fin.at[it, 1, sl[c]], left)
                d["sum", c] = copy(p.at[it, 3, sl[c]], fin.at[it, 0, sl[c]], right)
            else:
                d["relay", c] = copy(p.at[it, 2, sl[c]], rel.at[it, 0, sl[c]], left)
                d["own", c] = copy(p.at[it, 3, sl[c]], fin.at[it, 0, sl[c]], right)
                d["sum", c] = copy(p.at[it, 1, sl[c]], fin.at[it, 1, sl[c]], left)
        turns = [e for c in range(half) for e in (c, c + half)]
        apply_rows(it, 2, False)
        if last is not None:
            apply_rows(it, 3, False)
            apply_rows(it, 1, False)
            apply_rows(it, 0, False)
            last()
        for c in turns:
            d["relay", c].start()
        if last is None:
            apply_rows(it, 3, False)
            apply_rows(it, 1, False)
        for c in turns:
            d["own", c].start()
        if last is None:
            apply_rows(it, 0, False)
        for c in turns:
            d["relay", c].wait_recv()
            k = 3 if c < half else 1
            p[it, k, sl[c]] += rel[it, 0, sl[c]]
            d["sum", c].start()
        if last is not None:
            sum_middle(2)
        for c in turns:
            d["own", c].wait_recv()
            d["sum", c].wait_recv()
            yield sl[c], p[it, 0, sl[c]] + fin[it, 0, sl[c]] + fin[it, 1, sl[c]]

    def x_ring(i):
        return ring4(lambda k, h: gx.at[i, k, pl.ds(h * HR, HR)], 2, right, left)

    def send_w(it):
        d = y_ring(lambda c, k, h: wy.at[it, c, k, pl.ds(h * CR, CR)], CHUNKS)
        wy[it, 0, 0] += timed(((4, 5),))
        ring_start(d, CHUNKS)
        for h in range(CHUNKS):
            d["m", 0, h].start()
        return d


    def finish_w(it, d, stepped):
        split_w(it, 0, 0)
        mate_wait(d, CHUNKS, 0)
        split_w(it, 1, 0)
        if not stepped:
            ring_step1(d, CHUNKS, True)
        split_w(it, 0, 1)
        split_w(it, 0, 3)
        for k in (1, 3):
            mate_wait(d, CHUNKS, k)
            split_w(it, 1, k)
        for k in (2, 3, 1, 0):
            apply_rows(it, k, True)
        ring_step2(d, CHUNKS, True)
        split_w(it, 0, 2)
        mate_wait(d, CHUNKS, 2)
        split_w(it, 1, 2)

    ev = z_events(dz)
    split_field(0, zg[0, 0])
    build_left(0)
    build_right(0, 0)
    ring_step1(dfx, 2, False)
    ring_step1(dfy, 2, True)
    pump(ev, 1)
    build_left(1)
    build_left(3)
    make_kernel(0, 0, 0, 3)
    pump(ev, 1)
    mate_wait(dfy, 2, 0)
    build_right(1, 0)
    make_kernel(1, 0, 0, 3)
    pump(ev, 1)
    build_right(0, 1)
    make_kernel(0, 1, 0, 3)
    pump(ev, 1)
    ring_step2(dfx, 2, False)
    ring_step2(dfy, 2, True)
    dx = x_ring(0)
    ring_start(dx, 2)
    build_left(2)
    split_field(1, zg[0, 1])
    split_field(7, zg[0, 7])
    build_right(0, 3)
    make_kernel(0, 3, 0, 4)
    pump(ev, 1)
    make_kernel(0, 0, 3, 4)
    make_kernel(1, 0, 3, 4)
    make_kernel(0, 1, 3, 4)
    pump(ev, 1)
    build_right(0, 2)
    make_kernel(0, 2, 0, 4)
    pump(ev, 2)
    split_field(2, zg[0, 2])
    split_field(6, zg[0, 6])
    mate_wait(dfy, 2, 1)
    build_right(1, 1)
    make_kernel(1, 1, 0, 4)
    pump(ev, 1)
    ring_step1(dx, 2, False)
    mate_wait(dfy, 2, 3)
    build_right(1, 3)
    make_kernel(1, 3, 0, 4)
    pump(ev, 1)
    mate_wait(dfy, 2, 2)
    build_right(1, 2)
    make_kernel(1, 2, 0, 4)
    pump(ev, 2)
    ring_step2(dx, 2, False)
    split_field(3, zg[0, 3])
    split_field(5, zg[0, 5])
    timed_early(0)
    pump(ev, 2)
    split_field(4, zg[0, 4])
    dw = send_w(0)
    finish_w(0, dw, False)

    dz = z_ring(1)
    for i, (sl, total) in enumerate(spread(0, None)):
        q = mk[sl, :] * total + nz[sl, :] * gx[0, 0, sl]
        zg[1, 0, sl] = q
        gx[1, 0, sl] = q
        c = (i % 2) * CHUNKS // 2 + i // 2
        dz["RL"[i % 2], 1, c].start()
    for c in range(CHUNKS // 2):
        dz["R", 1, c + CHUNKS // 2].start()
        dz["L", 1, c].start()
    r0, q = zg[0, 0], zg[1, 0]
    sum_start(0, r0 * r0, r0 * q)
    dx = x_ring(1)
    ring_start(dx, 2)
    ev = z_events(dz)
    pump(ev, 3)
    sum_middle(0)
    pump(ev, 7)
    ring_step1(dx, 2, False)
    norm0, curv0 = sum_end(0)
    alpha = norm0 / curv0

    def residual_block(k):
        return zg[0, k] - alpha * zg[1, k]

    r1 = residual_block(0)
    sum_start(1, r1 * r1, r1)
    split_field(0, r1)
    for k in (1, 7, 2, 6):
        split_field(k, residual_block(k))
    pump(ev, 2)
    for k in (3, 5):
        split_field(k, residual_block(k))
    timed_early(1)
    pump(ev, 2)
    split_field(4, residual_block(4))
    dw = send_w(1)
    sum_middle(1)
    ring_step2(dx, 2, False)
    finish_w(1, dw, False)
    norm1, _ = sum_end(1)
    beta = norm1 / norm0

    def curvature():
        r1 = gx[0, 0] - alpha * gx[1, 0]
        d1 = r1 + beta * gx[0, 0]
        terms = d1 * (p[1, 0] + nz[...] * r1 + beta * gx[1, 0])
        for k in (1, 2, 3):
            terms += p[1, k] * (gx[0, k] - alpha * gx[1, k] + beta * gx[0, k])
        sum_start(2, terms, terms)

    for sl, total in spread(1, curvature):
        r1 = gx[0, 0, sl] - alpha * gx[1, 0, sl]
        res[sl, :] = mk[sl, :] * total + nz[sl, :] * r1 + beta * gx[1, 0, sl]
    curv1, _ = sum_end(2)
    alpha1 = norm1 / curv1
    r0 = gx[0, 0]
    r1 = r0 - alpha * gx[1, 0]
    sol[...] = alpha * r0 + alpha1 * (r1 + beta * r0)
    res[...] = r1 - alpha1 * res[...]

    for d in copies:
        d.wait_send()
    for n in range(3):
        whole(n, 0).wait_send()
        whole(n, 1).wait_send()


def body(targets, features, inv_scales, noise, time_kernel, block_mask):
    vmem = pl.BlockSpec(memory_space=pltpu.VMEM)
    block = jax.ShapeDtypeStruct((ROWS, COLS), F32)
    return pl.pallas_call(
        kernel,
        out_shape=(block, block),
        in_specs=[pl.BlockSpec(memory_space=pl.ANY)] * 6,
        out_specs=(vmem, vmem),
        scratch_shapes=[
            pltpu.VMEM((ROWS, COLS), F32),
            pltpu.VMEM((FEAT, ROWS), F32),
            pltpu.VMEM((1, FEAT), F32),
            pltpu.VMEM((1, ROWS), F32),
            pltpu.VMEM((COLS, NZ * COLS), F32),
            pltpu.VMEM((1, ROWS), jnp.int32),
            pltpu.SemaphoreType.DMA((6,)),
            pltpu.VMEM((2, NZ, ROWS, COLS), F32),
            pltpu.VMEM((2, NX, ROWS, COLS), F32),
            pltpu.VMEM((2, NCORE, NY, ROWS, COLS), F32),
            pltpu.VMEM((NCORE, NY, FEAT, ROWS), F32),
            pltpu.VMEM((NX, FEAT, ROWS), F32),
            pltpu.VMEM((NX * ROWS, DEPTH), BF16),
            pltpu.VMEM((DEPTH, 8 * ROWS), BF16),
            pltpu.VMEM((NX * ROWS, 16 * ROWS), BF16),
            pltpu.VMEM((8 * ROWS, 2 * COLS), BF16),
            pltpu.VMEM((ROWS, 2 * NZ * COLS), BF16),
            pltpu.VMEM((2 * COLS, NZ * COLS), BF16),
            pltpu.VMEM((2, NX, ROWS, COLS), F32),
            pltpu.VMEM((2, 1, ROWS, COLS), F32),
            pltpu.VMEM((2, 2, ROWS, COLS), F32),
            pltpu.VMEM((ROWS, COLS), F32),
            pltpu.VMEM((ROWS, COLS), F32),
            pltpu.VMEM((3, 2, 2, COLS), F32),
            pltpu.VMEM((3, PLANE - 1, 2, COLS), F32),
            pltpu.VMEM((3, NZ - 1, 2, COLS), F32),
            pltpu.SemaphoreType.DMA((NSEM,)),
            pltpu.SemaphoreType.DMA((NSEM,)),
            pltpu.SemaphoreType.DMA((3, 2)),
            pltpu.SemaphoreType.DMA((3, 2)),
        ],
        compiler_params=pltpu.CompilerParams(
            collective_id=0, has_side_effects=True, vmem_limit_bytes=67043328
        ),
    )(
        targets, features.T, inv_scales.reshape(1, FEAT), noise.reshape(1, ROWS), time_kernel, block_mask.T
    )


def solution(mesh):
    return jax.shard_map(
        body,
        mesh=mesh,
        in_specs=(P("cfg", "tm"), P("cfg", None), P(), P("cfg"), P("tm", None), P("cfg", "tm")),
        out_specs=(P("cfg", "tm"), P("cfg", "tm")),
        check_vma=False,
    )
```

```python
import math

import jax
import jax.numpy as jnp
from jax import lax
from jax.experimental import pallas as pl
from jax.experimental.pallas import tpu as pltpu
from jax.sharding import PartitionSpec as P

MESH = pl.DeviceIdType.MESH
F32, BF16 = jnp.float32, jnp.bfloat16
NY, NX, NCORE, NZ = 4, 4, 2, 8
PLANE = NY * NX * NCORE
ROWS, COLS, FEAT = 256, 128, 64
DEPTH = 384
CHUNKS = 4
NSEM = 256
UNIT = math.sqrt(3.0) * math.log2(math.e)
LN2 = math.log(2.0)
PLACE = (0, 1, 3, 2)


def split2(x):
    hi = x.astype(BF16)
    return hi, (x - hi.astype(F32)).astype(BF16)


def nt_dot(a, b):
    return lax.dot_general(a, b, (((1,), (1,)), ((), ())), preferred_element_type=F32)


def kernel(
    tgt_hbm, feat_hbm, isc_hbm, noise_hbm, tk_hbm, bm_hbm, sol, res,
    tgt, feat, isc, noise_ref, tk, bm, ins,
    zg, gx, wy, fy, fx, fl, fr, kc, wb, vb, tn, p, rel, fin, nz, mk,
    arsrc, arp, arz, ss, rs, ars, arr,
):
    me, z = lax.axis_index("cfg"), lax.axis_index("tm")
    core = lax.rem(me, NCORE)
    x = lax.rem(me // NCORE, NX)
    y = me // (NCORE * NX)

    def at(yy, xx, cc):
        return ((yy * NX + xx) * NCORE + cc, z)

    right, left = at(y, lax.rem(x + 1, NX), core), at(y, lax.rem(x + NX - 1, NX), core)
    up, down = at(lax.rem(y + 1, NY), x, core), at(lax.rem(y + NY - 1, NY), x, core)
    mate = at(y, x, 1 - core)
    zup, zdown = (me, lax.rem(z + 1, NZ)), (me, lax.rem(z + NZ - 1, NZ))
    plane = [(lax.rem(me + r, PLANE), z) for r in range(1, PLANE)]
    column = [(me, lax.rem(z + r, NZ)) for r in range(1, NZ)]

    copies = []

    def copy(src, dst, dev):
        i = len(copies)
        assert i < NSEM
        d = pltpu.make_async_remote_copy(
            src_ref=src, dst_ref=dst, send_sem=ss.at[i], recv_sem=rs.at[i],
            device_id=dev, device_id_type=MESH,
        )
        copies.append(d)
        return d

    pairs = ((bm_hbm, bm), (tgt_hbm, tgt), (isc_hbm, isc), (feat_hbm, feat), (noise_hbm, noise_ref), (tk_hbm, tk))
    loads = [pltpu.make_async_copy(a, b, ins.at[i]) for i, (a, b) in enumerate(pairs)]
    for d in loads:
        d.start()
    barrier = pltpu.get_barrier_semaphore()
    near = [mate, right, left, up, down, zup, zdown]
    for dev in near:
        pl.semaphore_signal(barrier, inc=1, device_id=dev, device_id_type=MESH)

    for d in loads[:4]:
        d.wait()
    mk[...] = jnp.broadcast_to(bm[...].astype(F32), (COLS, ROWS)).T
    r0 = mk[...] * tgt[...]
    zg[0, 0] = r0
    gx[0, 0] = r0
    fscaled = feat[...] * (isc[...].T * UNIT)
    fy[0, 0] = fscaled
    fx[0] = fscaled

    pl.semaphore_wait(barrier, len(near))

    def ring4(buf, nh, fwd, back):
        d = {}
        for h in range(nh):
            d["R1", h] = copy(buf(0, h), buf(1, h), fwd)
            d["L1", h] = copy(buf(0, h), buf(3, h), back)
        for h in range(nh):
            if h < nh // 2:
                d["2", h] = copy(buf(1, h), buf(2, h), fwd)
            else:
                d["2", h] = copy(buf(3, h), buf(2, h), back)
        return d

    def y_ring(buf, nh):
        d = ring4(lambda k, h: buf(0, k, h), nh, up, down)
        for k in (0, 1, 3, 2):
            for h in range(nh):
                d["m", k, h] = copy(buf(0, k, h), buf(1, k, h), mate)
        return d

    def order(nh):
        return [(h, (h + nh // 2) % nh) for h in range(nh)]

    def ring_start(d, nh):
        for h, g in order(nh):
            d["R1", h].start()
            d["L1", g].start()

    def ring_step1(d, nh, mated):
        for h, g in order(nh):
            d["R1", h].wait_recv()
            if h < nh // 2:
                d["2", h].start()
            d["L1", g].wait_recv()
            if g >= nh // 2:
                d["2", g].start()
            if mated:
                d["m", 1, h].start()
                d["m", 3, g].start()

    def ring_step2(d, nh, mated):
        for h, g in order(nh)[: nh // 2]:
            for e in (h, g):
                d["2", e].wait_recv()
                if mated:
                    d["m", 2, e].start()

    def mate_wait(d, nh, k):
        for h in range(nh):
            d["m", k, h].wait_recv()

    CR = ROWS // CHUNKS

    def z_ring(it):
        d = {}
        for s in range(1, 5):
            for c in range(CHUNKS):
                sl = pl.ds(c * CR, CR)
                if s < 4 or c < CHUNKS // 2:
                    d["R", s, c] = copy(zg.at[it, s - 1, sl], zg.at[it, s, sl], zup)
                if s < 4 or c >= CHUNKS // 2:
                    d["L", s, c] = copy(zg.at[it, (9 - s) % 8, sl], zg.at[it, 8 - s, sl], zdown)
        return d

    def z_start(d, c):
        d["R", 1, c].start()
        d["L", 1, (c + CHUNKS // 2) % CHUNKS].start()

    def z_events(d):
        for s in range(1, 5):
            for c in range(CHUNKS if s < 4 else CHUNKS // 2):
                for way, e in (("R", c), ("L", (c + CHUNKS // 2) % CHUNKS)):
                    d[way, s, e].wait_recv()
                    if (way, s + 1, e) in d:
                        d[way, s + 1, e].start()
                yield

    def pump(events, n):
        for _ in range(n):
            next(events)

    def plane_copies(n):
        return [
            pltpu.make_async_remote_copy(
                src_ref=arsrc.at[n, 0], dst_ref=arp.at[n, r], send_sem=ars.at[n, 0], recv_sem=arr.at[n, 0],
                device_id=dev, device_id_type=MESH,
            )
            for r, dev in enumerate(plane)
        ]

    def column_copies(n):
        return [
            pltpu.make_async_remote_copy(
                src_ref=arsrc.at[n, 1], dst_ref=arz.at[n, r], send_sem=ars.at[n, 1], recv_sem=arr.at[n, 1],
                device_id=dev, device_id_type=MESH,
            )
            for r, dev in enumerate(column)
        ]

    def whole(n, j):
        buf, dev = (arp, plane[0]) if j == 0 else (arz, column[0])
        return pltpu.make_async_remote_copy(
            src_ref=buf.at[n], dst_ref=buf.at[n], send_sem=ars.at[n, j], recv_sem=arr.at[n, j],
            device_id=dev, device_id_type=MESH,
        )

    def sum_start(n, first, second):
        arsrc[n, 0, 0:1] = jnp.sum(first, axis=0, keepdims=True)
        arsrc[n, 0, 1:2] = jnp.sum(second, axis=0, keepdims=True)
        for d in plane_copies(n):
            d.start()

    def sum_middle(n):
        whole(n, 0).wait_recv()
        arsrc[n, 1] = arsrc[n, 0] + jnp.sum(arp[n], axis=0)
        for d in column_copies(n):
            d.start()

    def sum_end(n):
        whole(n, 1).wait_recv()
        both = arsrc[n, 1] + jnp.sum(arz[n], axis=0)
        both = jnp.sum(both, axis=1, keepdims=True)
        return both[0:1], both[1:2]

    dz = z_ring(0)
    for c in range(CHUNKS):
        z_start(dz, c)
    FH = ROWS // 2
    dfx = ring4(lambda k, h: fx.at[k, :, pl.ds(h * FH, FH)], 2, right, left)
    dfy = y_ring(lambda c, k, h: fy.at[c, k, :, pl.ds(h * FH, FH)], 2)
    ring_start(dfy, 2)
    ring_start(dfx, 2)
    for h in range(2):
        dfy["m", 0, h].start()

    loads[4].wait()
    nz[...] = jnp.broadcast_to(noise_ref[...], (COLS, ROWS)).T
    loads[5].wait()
    for k in range(NZ):
        o = lax.rem(z + NZ - k, NZ)
        hi, lo = split2(tk[:, pl.ds(pl.multiple_of(o * COLS, COLS), COLS)])
        tn[0:COLS, k * COLS : (k + 1) * COLS] = hi
        tn[COLS : 2 * COLS, k * COLS : (k + 1) * COLS] = lo

    def parts(block):
        hi = block.astype(BF16).astype(F32)
        lo = (block - hi).astype(BF16).astype(F32)
        kept = hi + lo
        n = jnp.sum(kept * kept, axis=0, keepdims=True)
        n1 = n.astype(BF16).astype(F32)
        n2 = (n - n1).astype(BF16).astype(F32)
        return hi, lo, jnp.concatenate([n1, n2, n - n1 - n2], axis=0)

    pad = DEPTH - 4 * FEAT
    row = lax.broadcasted_iota(jnp.int32, (pad, ROWS), 0)

    def place(n, first):
        out = jnp.where((row >= 3 - first) & (row < 6 - first), 1.0, 0.0)
        for i in range(3):
            out = jnp.where(row == first + i, jnp.broadcast_to(n[i : i + 1], (pad, ROWS)), out)
        return out

    def build_left(k):
        hi, lo, n = parts(fx[k])
        stack = jnp.concatenate([-2.0 * hi, -2.0 * hi, -2.0 * lo, -2.0 * lo, place(n, 0)], axis=0)
        i = PLACE[k]
        fl[i * ROWS : (i + 1) * ROWS, :] = stack.T.astype(BF16)

    def build_right(c, k):
        hi, lo, n = parts(fy[c, k])
        stack = jnp.concatenate([hi, lo, hi, lo, place(n, 3)], axis=0)
        j = c * NY + k
        fr[:, j * ROWS : (j + 1) * ROWS] = stack.astype(BF16)

    def make_kernel(c, k, first, end):
        j = c * NY + k
        cols = slice(j * ROWS, (j + 1) * ROWS)
        low = slice((8 + j) * ROWS, (9 + j) * ROWS)

        def one(i):
            sl = slice(i * ROWS, (i + 1) * ROWS)
            d2 = jnp.dot(fl[sl, :], fr[:, cols], preferred_element_type=F32)
            d2 = jnp.maximum(d2, 1e-30)
            u = d2 * lax.rsqrt(d2)
            value = (1.0 + LN2 * u) * jnp.exp2(-u)
            hi, lo = split2(value)
            kc[sl, cols] = hi
            kc[sl, low] = lo

        for i in range(first, end):
            one(i)

    def split_field(k, block):
        hi, lo = split2(block)
        vb[:, k * COLS : (k + 1) * COLS] = hi
        vb[:, (NZ + k) * COLS : (NZ + k + 1) * COLS] = lo

    def timed(spans):
        acc = None
        for off in (0, NZ):
            for lo, hi in spans:
                part = nt_dot(vb[:, (off + lo) * COLS : (off + hi) * COLS], tn[:, lo * COLS : hi * COLS])
                acc = part if acc is None else acc + part
        return acc[:, :COLS] + acc[:, COLS:]

    def timed_early(it):
        wy[it, 0, 0] = timed(((0, 4), (5, 8)))

    def split_w(it, c, k):
        hi, lo = split2(wy[it, c, k])
        j = c * NY + k
        wb[j * ROWS : (j + 1) * ROWS, :COLS] = hi
        wb[j * ROWS : (j + 1) * ROWS, COLS:] = lo

    def apply_rows(it, k, early):
        n = ROWS
        sl = slice(PLACE[k] * n, (PLACE[k] + 1) * n)
        acc = None
        for lo, hi in ((0, 2), (3, 6), (7, 8)) if early else ((2, 3), (6, 7)):
            for off in (0, 8):
                part = jnp.dot(kc[sl, (off + lo) * n : (off + hi) * n], wb[lo * n : hi * n, :], preferred_element_type=F32)
                acc = part if acc is None else acc + part
        out = acc[:, :COLS] + acc[:, COLS:]
        if early:
            p[it, k] = out
        else:
            p[it, k] += out

    HR = ROWS // 2
    A, B = pl.ds(0, HR), pl.ds(HR, HR)

    def spread(it, last, nc):
        half, size = nc // 2, ROWS // nc
        sl = [pl.ds(c * size, size) for c in range(nc)]
        d = {}
        for c in range(nc):
            if c < half:
                d["relay", c] = copy(p.at[it, 2, sl[c]], rel.at[it, 0, sl[c]], right)
                d["own", c] = copy(p.at[it, 1, sl[c]], fin.at[it, 1, sl[c]], left)
                d["sum", c] = copy(p.at[it, 3, sl[c]], fin.at[it, 0, sl[c]], right)
            else:
                d["relay", c] = copy(p.at[it, 2, sl[c]], rel.at[it, 0, sl[c]], left)
                d["own", c] = copy(p.at[it, 3, sl[c]], fin.at[it, 0, sl[c]], right)
                d["sum", c] = copy(p.at[it, 1, sl[c]], fin.at[it, 1, sl[c]], left)
        turns = [e for c in range(half) for e in (c, c + half)]
        apply_rows(it, 2, False)
        if last is not None:
            apply_rows(it, 3, False)
            apply_rows(it, 1, False)
            apply_rows(it, 0, False)
            last()
        for c in turns:
            d["relay", c].start()
        if last is None:
            apply_rows(it, 3, False)
            apply_rows(it, 1, False)
        for c in turns:
            d["own", c].start()
        if last is None:
            apply_rows(it, 0, False)
        for c in turns:
            d["relay", c].wait_recv()
            k = 3 if c < half else 1
            p[it, k, sl[c]] += rel[it, 0, sl[c]]
            d["sum", c].start()
        if last is not None:
            sum_middle(2)
        for c in turns:
            d["own", c].wait_recv()
            d["sum", c].wait_recv()
            yield sl[c], p[it, 0, sl[c]] + fin[it, 0, sl[c]] + fin[it, 1, sl[c]]

    def x_ring(i):
        return ring4(lambda k, h: gx.at[i, k, pl.ds(h * HR, HR)], 2, right, left)

    def send_w(it):
        d = y_ring(lambda c, k, h: wy.at[it, c, k, pl.ds(h * HR, HR)], 2)
        wy[it, 0, 0] += timed(((4, 5),))
        ring_start(d, 2)
        for h in range(2):
            d["m", 0, h].start()
        return d


    def finish_w(it, d, stepped):
        split_w(it, 0, 0)
        mate_wait(d, 2, 0)
        split_w(it, 1, 0)
        if not stepped:
            ring_step1(d, 2, True)
        split_w(it, 0, 1)
        split_w(it, 0, 3)
        for k in (1, 3):
            mate_wait(d, 2, k)
            split_w(it, 1, k)
        for k in (2, 3, 1, 0):
            apply_rows(it, k, True)
        ring_step2(d, 2, True)
        split_w(it, 0, 2)
        mate_wait(d, 2, 2)
        split_w(it, 1, 2)

    ev = z_events(dz)
    split_field(0, zg[0, 0])
    build_left(0)
    build_right(0, 0)
    ring_step1(dfx, 2, False)
    ring_step1(dfy, 2, True)
    pump(ev, 1)
    build_left(1)
    build_left(3)
    make_kernel(0, 0, 0, 3)
    pump(ev, 1)
    mate_wait(dfy, 2, 0)
    build_right(1, 0)
    make_kernel(1, 0, 0, 3)
    pump(ev, 1)
    build_right(0, 1)
    make_kernel(0, 1, 0, 3)
    pump(ev, 1)
    ring_step2(dfx, 2, False)
    ring_step2(dfy, 2, True)
    build_left(2)
    split_field(1, zg[0, 1])
    split_field(7, zg[0, 7])
    build_right(0, 3)
    make_kernel(0, 3, 0, 4)
    pump(ev, 1)
    make_kernel(0, 0, 3, 4)
    make_kernel(1, 0, 3, 4)
    make_kernel(0, 1, 3, 4)
    pump(ev, 1)
    build_right(0, 2)
    make_kernel(0, 2, 0, 4)
    pump(ev, 2)
    split_field(2, zg[0, 2])
    split_field(6, zg[0, 6])
    mate_wait(dfy, 2, 1)
    build_right(1, 1)
    make_kernel(1, 1, 0, 4)
    pump(ev, 1)
    mate_wait(dfy, 2, 3)
    build_right(1, 3)
    make_kernel(1, 3, 0, 4)
    pump(ev, 1)
    mate_wait(dfy, 2, 2)
    build_right(1, 2)
    make_kernel(1, 2, 0, 4)
    pump(ev, 2)
    split_field(3, zg[0, 3])
    split_field(5, zg[0, 5])
    timed_early(0)
    pump(ev, 2)
    split_field(4, zg[0, 4])
    dw = send_w(0)
    finish_w(0, dw, False)

    dz = z_ring(1)
    for i, (sl, total) in enumerate(spread(0, None, CHUNKS)):
        q = mk[sl, :] * total + nz[sl, :] * gx[0, 0, sl]
        zg[1, 0, sl] = q
        gx[1, 0, sl] = q
        c = (i % 2) * CHUNKS // 2 + i // 2
        dz["RL"[i % 2], 1, c].start()
    for c in range(CHUNKS // 2):
        dz["R", 1, c + CHUNKS // 2].start()
        dz["L", 1, c].start()
    r0, q = zg[0, 0], zg[1, 0]
    sum_start(0, r0 * r0, r0 * q)
    dx, dx0 = x_ring(1), x_ring(0)
    ring_start(dx, 2)
    ring_start(dx0, 2)
    ev = z_events(dz)
    pump(ev, 3)
    sum_middle(0)
    pump(ev, 7)
    ring_step1(dx, 2, False)
    ring_step1(dx0, 2, False)
    norm0, curv0 = sum_end(0)
    alpha = norm0 / curv0

    def residual_block(k):
        return zg[0, k] - alpha * zg[1, k]

    r1 = residual_block(0)
    sum_start(1, r1 * r1, r1)
    split_field(0, r1)
    for k in (1, 7, 2, 6):
        split_field(k, residual_block(k))
    pump(ev, 2)
    for k in (3, 5):
        split_field(k, residual_block(k))
    timed_early(1)
    pump(ev, 2)
    split_field(4, residual_block(4))
    dw = send_w(1)
    sum_middle(1)
    ring_step2(dx, 2, False)
    ring_step2(dx0, 2, False)
    finish_w(1, dw, False)
    norm1, _ = sum_end(1)
    beta = norm1 / norm0

    def curvature():
        r1 = gx[0, 0] - alpha * gx[1, 0]
        d1 = r1 + beta * gx[0, 0]
        terms = d1 * (p[1, 0] + nz[...] * r1 + beta * gx[1, 0])
        for k in (1, 2, 3):
            terms += p[1, k] * (gx[0, k] - alpha * gx[1, k] + beta * gx[0, k])
        sum_start(2, terms, terms)

    for sl, total in spread(1, curvature, 2):
        r1 = gx[0, 0, sl] - alpha * gx[1, 0, sl]
        res[sl, :] = mk[sl, :] * total + nz[sl, :] * r1 + beta * gx[1, 0, sl]
    curv1, _ = sum_end(2)
    alpha1 = norm1 / curv1
    r0 = gx[0, 0]
    r1 = r0 - alpha * gx[1, 0]
    sol[...] = alpha * r0 + alpha1 * (r1 + beta * r0)
    res[...] = r1 - alpha1 * res[...]

    for d in copies:
        d.wait_send()
    for n in range(3):
        whole(n, 0).wait_send()
        whole(n, 1).wait_send()


def body(targets, features, inv_scales, noise, time_kernel, block_mask):
    vmem = pl.BlockSpec(memory_space=pltpu.VMEM)
    block = jax.ShapeDtypeStruct((ROWS, COLS), F32)
    return pl.pallas_call(
        kernel,
        out_shape=(block, block),
        in_specs=[pl.BlockSpec(memory_space=pl.ANY)] * 6,
        out_specs=(vmem, vmem),
        scratch_shapes=[
            pltpu.VMEM((ROWS, COLS), F32),
            pltpu.VMEM((FEAT, ROWS), F32),
            pltpu.VMEM((1, FEAT), F32),
            pltpu.VMEM((1, ROWS), F32),
            pltpu.VMEM((COLS, NZ * COLS), F32),
            pltpu.VMEM((1, ROWS), jnp.int32),
            pltpu.SemaphoreType.DMA((6,)),
            pltpu.VMEM((2, NZ, ROWS, COLS), F32),
            pltpu.VMEM((2, NX, ROWS, COLS), F32),
            pltpu.VMEM((2, NCORE, NY, ROWS, COLS), F32),
            pltpu.VMEM((NCORE, NY, FEAT, ROWS), F32),
            pltpu.VMEM((NX, FEAT, ROWS), F32),
            pltpu.VMEM((NX * ROWS, DEPTH), BF16),
            pltpu.VMEM((DEPTH, 8 * ROWS), BF16),
            pltpu.VMEM((NX * ROWS, 16 * ROWS), BF16),
            pltpu.VMEM((8 * ROWS, 2 * COLS), BF16),
            pltpu.VMEM((ROWS, 2 * NZ * COLS), BF16),
            pltpu.VMEM((2 * COLS, NZ * COLS), BF16),
            pltpu.VMEM((2, NX, ROWS, COLS), F32),
            pltpu.VMEM((2, 1, ROWS, COLS), F32),
            pltpu.VMEM((2, 2, ROWS, COLS), F32),
            pltpu.VMEM((ROWS, COLS), F32),
            pltpu.VMEM((ROWS, COLS), F32),
            pltpu.VMEM((3, 2, 2, COLS), F32),
            pltpu.VMEM((3, PLANE - 1, 2, COLS), F32),
            pltpu.VMEM((3, NZ - 1, 2, COLS), F32),
            pltpu.SemaphoreType.DMA((NSEM,)),
            pltpu.SemaphoreType.DMA((NSEM,)),
            pltpu.SemaphoreType.DMA((3, 2)),
            pltpu.SemaphoreType.DMA((3, 2)),
        ],
        compiler_params=pltpu.CompilerParams(
            collective_id=0, has_side_effects=True, vmem_limit_bytes=67043328
        ),
    )(
        targets, features.T, inv_scales.reshape(1, FEAT), noise.reshape(1, ROWS), time_kernel, block_mask.T
    )


def solution(mesh):
    return jax.shard_map(
        body,
        mesh=mesh,
        in_specs=(P("cfg", "tm"), P("cfg", None), P(), P("cfg"), P("tm", None), P("cfg", "tm")),
        out_specs=(P("cfg", "tm"), P("cfg", "tm")),
        check_vma=False,
    )
```

```python
import math

import jax
import jax.numpy as jnp
from jax import lax
from jax.experimental import pallas as pl
from jax.experimental.pallas import tpu as pltpu
from jax.sharding import PartitionSpec as P

MESH = pl.DeviceIdType.MESH
F32, BF16 = jnp.float32, jnp.bfloat16
NY, NX, NCORE, NZ = 4, 4, 2, 8
PLANE = NY * NX * NCORE
ROWS, COLS, FEAT = 256, 128, 64
DEPTH = 384
CHUNKS = 4
NSEM = 256
UNIT = math.sqrt(3.0) * math.log2(math.e)
LN2 = math.log(2.0)
PLACE = (0, 1, 3, 2)


def split2(x):
    hi = x.astype(BF16)
    return hi, (x - hi.astype(F32)).astype(BF16)


def nt_dot(a, b):
    return lax.dot_general(a, b, (((1,), (1,)), ((), ())), preferred_element_type=F32)


def kernel(
    tgt_hbm, feat_hbm, isc_hbm, noise_hbm, tk_hbm, bm_hbm, sol, res,
    tgt, feat, isc, noise_ref, tk, bm, ins,
    zg, gx, wy, fy, fx, fl, fr, kc, wb, vb, tn, p, rel, fin, nz, mk,
    arsrc, arp, arz, ss, rs, ars, arr,
):
    me, z = lax.axis_index("cfg"), lax.axis_index("tm")
    core = lax.rem(me, NCORE)
    x = lax.rem(me // NCORE, NX)
    y = me // (NCORE * NX)

    def at(yy, xx, cc):
        return ((yy * NX + xx) * NCORE + cc, z)

    right, left = at(y, lax.rem(x + 1, NX), core), at(y, lax.rem(x + NX - 1, NX), core)
    up, down = at(lax.rem(y + 1, NY), x, core), at(lax.rem(y + NY - 1, NY), x, core)
    mate = at(y, x, 1 - core)
    zup, zdown = (me, lax.rem(z + 1, NZ)), (me, lax.rem(z + NZ - 1, NZ))
    plane = [(lax.rem(me + r, PLANE), z) for r in range(1, PLANE)]
    column = [(me, lax.rem(z + r, NZ)) for r in range(1, NZ)]

    copies = []

    def copy(src, dst, dev):
        i = len(copies)
        assert i < NSEM
        d = pltpu.make_async_remote_copy(
            src_ref=src, dst_ref=dst, send_sem=ss.at[i], recv_sem=rs.at[i],
            device_id=dev, device_id_type=MESH,
        )
        copies.append(d)
        return d

    pairs = ((bm_hbm, bm), (tgt_hbm, tgt), (isc_hbm, isc), (feat_hbm, feat), (noise_hbm, noise_ref), (tk_hbm, tk))
    loads = [pltpu.make_async_copy(a, b, ins.at[i]) for i, (a, b) in enumerate(pairs)]
    for d in loads:
        d.start()
    barrier = pltpu.get_barrier_semaphore()
    near = [mate, right, left, up, down, zup, zdown]
    for dev in near:
        pl.semaphore_signal(barrier, inc=1, device_id=dev, device_id_type=MESH)

    for d in loads[:4]:
        d.wait()
    mk[...] = jnp.broadcast_to(bm[...].astype(F32), (COLS, ROWS)).T
    r0 = mk[...] * tgt[...]
    zg[0, 0] = r0
    gx[0, 0] = r0
    fscaled = feat[...] * (isc[...].T * UNIT)
    fy[0, 0] = fscaled
    fx[0] = fscaled

    pl.semaphore_wait(barrier, len(near))

    def ring4(buf, nh, fwd, back):
        d = {}
        for h in range(nh):
            d["R1", h] = copy(buf(0, h), buf(1, h), fwd)
            d["L1", h] = copy(buf(0, h), buf(3, h), back)
        for h in range(nh):
            if h < nh // 2:
                d["2", h] = copy(buf(1, h), buf(2, h), fwd)
            else:
                d["2", h] = copy(buf(3, h), buf(2, h), back)
        return d

    def y_ring(buf, nh, own):
        d = ring4(lambda k, h: buf(0, k, h), nh, up, down)
        d["m", 0, 0] = copy(*own, mate)
        for k in (1, 3, 2):
            for h in range(nh):
                d["m", k, h] = copy(buf(0, k, h), buf(1, k, h), mate)
        return d

    def order(nh):
        return [(h, (h + nh // 2) % nh) for h in range(nh)]

    def ring_start(d, nh):
        for h, g in order(nh):
            d["R1", h].start()
            d["L1", g].start()

    def ring_step1(d, nh, mated):
        for h, g in order(nh):
            d["R1", h].wait_recv()
            if h < nh // 2:
                d["2", h].start()
            d["L1", g].wait_recv()
            if g >= nh // 2:
                d["2", g].start()
            if mated:
                d["m", 1, h].start()
                d["m", 3, g].start()

    def ring_step2(d, nh, mated):
        for h, g in order(nh)[: nh // 2]:
            for e in (h, g):
                d["2", e].wait_recv()
                if mated:
                    d["m", 2, e].start()

    def mate_wait(d, nh, k):
        for h in range(nh if k else 1):
            d["m", k, h].wait_recv()

    CR = ROWS // CHUNKS

    def z_ring(it):
        d = {}
        for s in range(1, 5):
            for c in range(CHUNKS):
                sl = pl.ds(c * CR, CR)
                if s < 4 or c < CHUNKS // 2:
                    d["R", s, c] = copy(zg.at[it, s - 1, sl], zg.at[it, s, sl], zup)
                if s < 4 or c >= CHUNKS // 2:
                    d["L", s, c] = copy(zg.at[it, (9 - s) % 8, sl], zg.at[it, 8 - s, sl], zdown)
        return d

    def z_start(d, c):
        d["R", 1, c].start()
        d["L", 1, (c + CHUNKS // 2) % CHUNKS].start()

    def z_events(d):
        for s in range(1, 5):
            for c in range(CHUNKS if s < 4 else CHUNKS // 2):
                for way, e in (("R", c), ("L", (c + CHUNKS // 2) % CHUNKS)):
                    d[way, s, e].wait_recv()
                    if (way, s + 1, e) in d:
                        d[way, s + 1, e].start()
                yield

    def pump(events, n):
        for _ in range(n):
            next(events)

    def plane_copies(n):
        return [
            pltpu.make_async_remote_copy(
                src_ref=arsrc.at[n, 0], dst_ref=arp.at[n, r], send_sem=ars.at[n, 0], recv_sem=arr.at[n, 0],
                device_id=dev, device_id_type=MESH,
            )
            for r, dev in enumerate(plane)
        ]

    def column_copies(n):
        return [
            pltpu.make_async_remote_copy(
                src_ref=arsrc.at[n, 1], dst_ref=arz.at[n, r], send_sem=ars.at[n, 1], recv_sem=arr.at[n, 1],
                device_id=dev, device_id_type=MESH,
            )
            for r, dev in enumerate(column)
        ]

    def whole(n, j):
        buf, dev = (arp, plane[0]) if j == 0 else (arz, column[0])
        return pltpu.make_async_remote_copy(
            src_ref=buf.at[n], dst_ref=buf.at[n], send_sem=ars.at[n, j], recv_sem=arr.at[n, j],
            device_id=dev, device_id_type=MESH,
        )

    def sum_start(n, first, second):
        arsrc[n, 0, 0:1] = jnp.sum(first, axis=0, keepdims=True)
        arsrc[n, 0, 1:2] = jnp.sum(second, axis=0, keepdims=True)
        for d in plane_copies(n):
            d.start()

    def sum_middle(n):
        whole(n, 0).wait_recv()
        arsrc[n, 1] = arsrc[n, 0] + jnp.sum(arp[n], axis=0)
        for d in column_copies(n):
            d.start()

    def sum_end(n):
        whole(n, 1).wait_recv()
        both = arsrc[n, 1] + jnp.sum(arz[n], axis=0)
        both = jnp.sum(both, axis=1, keepdims=True)
        return both[0:1], both[1:2]

    dz = z_ring(0)
    for c in range(CHUNKS):
        z_start(dz, c)
    FH = ROWS // 2
    dfx = ring4(lambda k, h: fx.at[k, :, pl.ds(h * FH, FH)], 2, right, left)
    dfy = y_ring(lambda c, k, h: fy.at[c, k, :, pl.ds(h * FH, FH)], 2, (fy.at[0, 0], fy.at[1, 0]))
    ring_start(dfy, 2)
    ring_start(dfx, 2)
    dfy["m", 0, 0].start()

    loads[4].wait()
    nz[...] = jnp.broadcast_to(noise_ref[...], (COLS, ROWS)).T
    loads[5].wait()
    for k in range(NZ):
        o = lax.rem(z + NZ - k, NZ)
        hi, lo = split2(tk[:, pl.ds(pl.multiple_of(o * COLS, COLS), COLS)])
        tn[0:COLS, k * COLS : (k + 1) * COLS] = hi
        tn[COLS : 2 * COLS, k * COLS : (k + 1) * COLS] = lo

    def parts(block):
        hi = block.astype(BF16).astype(F32)
        lo = (block - hi).astype(BF16).astype(F32)
        kept = hi + lo
        n = jnp.sum(kept * kept, axis=0, keepdims=True)
        n1 = n.astype(BF16).astype(F32)
        n2 = (n - n1).astype(BF16).astype(F32)
        return hi, lo, jnp.concatenate([n1, n2, n - n1 - n2], axis=0)

    pad = DEPTH - 4 * FEAT
    row = lax.broadcasted_iota(jnp.int32, (pad, ROWS), 0)

    def place(n, first):
        out = jnp.where((row >= 3 - first) & (row < 6 - first), 1.0, 0.0)
        for i in range(3):
            out = jnp.where(row == first + i, jnp.broadcast_to(n[i : i + 1], (pad, ROWS)), out)
        return out

    def build_left(k):
        hi, lo, n = parts(fx[k])
        stack = jnp.concatenate([-2.0 * hi, -2.0 * hi, -2.0 * lo, -2.0 * lo, place(n, 0)], axis=0)
        i = PLACE[k]
        fl[i * ROWS : (i + 1) * ROWS, :] = stack.T.astype(BF16)

    def build_right(c, k):
        hi, lo, n = parts(fy[c, k])
        stack = jnp.concatenate([hi, lo, hi, lo, place(n, 3)], axis=0)
        j = c * NY + k
        fr[:, j * ROWS : (j + 1) * ROWS] = stack.astype(BF16)

    def make_kernel(c, k, first, end):
        j = c * NY + k
        cols = slice(j * ROWS, (j + 1) * ROWS)
        low = slice((8 + j) * ROWS, (9 + j) * ROWS)

        def one(i):
            sl = slice(i * ROWS, (i + 1) * ROWS)
            d2 = jnp.dot(fl[sl, :], fr[:, cols], preferred_element_type=F32)
            d2 = jnp.maximum(d2, 1e-30)
            u = d2 * lax.rsqrt(d2)
            value = (1.0 + LN2 * u) * jnp.exp2(-u)
            hi, lo = split2(value)
            kc[sl, cols] = hi
            kc[sl, low] = lo

        for i in range(first, end):
            one(i)

    def split_field(k, block):
        hi, lo = split2(block)
        vb[:, k * COLS : (k + 1) * COLS] = hi
        vb[:, (NZ + k) * COLS : (NZ + k + 1) * COLS] = lo

    def timed(spans):
        acc = None
        for off in (0, NZ):
            for lo, hi in spans:
                part = nt_dot(vb[:, (off + lo) * COLS : (off + hi) * COLS], tn[:, lo * COLS : hi * COLS])
                acc = part if acc is None else acc + part
        return acc[:, :COLS] + acc[:, COLS:]

    def timed_early(it):
        wy[it, 0, 0] = timed(((0, 4), (5, 8)))

    def split_w(it, c, k):
        hi, lo = split2(wy[it, c, k])
        j = c * NY + k
        wb[j * ROWS : (j + 1) * ROWS, :COLS] = hi
        wb[j * ROWS : (j + 1) * ROWS, COLS:] = lo

    def apply_rows(it, k, early):
        n = ROWS
        sl = slice(PLACE[k] * n, (PLACE[k] + 1) * n)
        acc = None
        for lo, hi in ((0, 2), (3, 6), (7, 8)) if early else ((2, 3), (6, 7)):
            for off in (0, 8):
                part = jnp.dot(kc[sl, (off + lo) * n : (off + hi) * n], wb[lo * n : hi * n, :], preferred_element_type=F32)
                acc = part if acc is None else acc + part
        out = acc[:, :COLS] + acc[:, COLS:]
        if early:
            p[it, k] = out
        else:
            p[it, k] += out

    HR = ROWS // 2
    A, B = pl.ds(0, HR), pl.ds(HR, HR)

    def spread(it, last, nc):
        half, size = nc // 2, ROWS // nc
        sl = [pl.ds(c * size, size) for c in range(nc)]
        d = {}
        for c in range(nc):
            if c < half:
                d["relay", c] = copy(p.at[it, 2, sl[c]], rel.at[it, 0, sl[c]], right)
                d["own", c] = copy(p.at[it, 1, sl[c]], fin.at[it, 1, sl[c]], left)
                d["sum", c] = copy(p.at[it, 3, sl[c]], fin.at[it, 0, sl[c]], right)
            else:
                d["relay", c] = copy(p.at[it, 2, sl[c]], rel.at[it, 0, sl[c]], left)
                d["own", c] = copy(p.at[it, 3, sl[c]], fin.at[it, 0, sl[c]], right)
                d["sum", c] = copy(p.at[it, 1, sl[c]], fin.at[it, 1, sl[c]], left)
        turns = [e for c in range(half) for e in (c, c + half)]
        apply_rows(it, 2, False)
        if last is not None:
            apply_rows(it, 3, False)
            apply_rows(it, 1, False)
            apply_rows(it, 0, False)
            last()
        for c in turns:
            d["relay", c].start()
        if last is None:
            apply_rows(it, 3, False)
            apply_rows(it, 1, False)
        for c in turns:
            d["own", c].start()
        if last is None:
            apply_rows(it, 0, False)
        for c in turns:
            d["relay", c].wait_recv()
            k = 3 if c < half else 1
            p[it, k, sl[c]] += rel[it, 0, sl[c]]
            d["sum", c].start()
        if last is not None:
            sum_middle(2)
        for c in turns:
            d["own", c].wait_recv()
            d["sum", c].wait_recv()
            yield sl[c], p[it, 0, sl[c]] + fin[it, 0, sl[c]] + fin[it, 1, sl[c]]

    def x_ring(i):
        return ring4(lambda k, h: gx.at[i, k, pl.ds(h * HR, HR)], 2, right, left)

    def send_w(it):
        d = y_ring(lambda c, k, h: wy.at[it, c, k, pl.ds(h * HR, HR)], 2, (wy.at[it, 0, 0], wy.at[it, 1, 0]))
        wy[it, 0, 0] += timed(((4, 5),))
        ring_start(d, 2)
        d["m", 0, 0].start()
        return d


    def finish_w(it, d, stepped):
        split_w(it, 0, 0)
        mate_wait(d, 2, 0)
        split_w(it, 1, 0)
        if not stepped:
            ring_step1(d, 2, True)
        split_w(it, 0, 1)
        split_w(it, 0, 3)
        for k in (1, 3):
            mate_wait(d, 2, k)
            split_w(it, 1, k)
        for k in (2, 3, 1, 0):
            apply_rows(it, k, True)
        ring_step2(d, 2, True)
        split_w(it, 0, 2)
        mate_wait(d, 2, 2)
        split_w(it, 1, 2)

    ev = z_events(dz)
    split_field(0, zg[0, 0])
    build_left(0)
    build_right(0, 0)
    ring_step1(dfx, 2, False)
    ring_step1(dfy, 2, True)
    pump(ev, 1)
    build_left(1)
    build_left(3)
    make_kernel(0, 0, 0, 3)
    pump(ev, 1)
    mate_wait(dfy, 2, 0)
    build_right(1, 0)
    make_kernel(1, 0, 0, 3)
    pump(ev, 1)
    build_right(0, 1)
    make_kernel(0, 1, 0, 3)
    pump(ev, 1)
    ring_step2(dfx, 2, False)
    ring_step2(dfy, 2, True)
    build_left(2)
    split_field(1, zg[0, 1])
    split_field(7, zg[0, 7])
    build_right(0, 3)
    make_kernel(0, 3, 0, 4)
    pump(ev, 1)
    make_kernel(0, 0, 3, 4)
    make_kernel(1, 0, 3, 4)
    make_kernel(0, 1, 3, 4)
    pump(ev, 1)
    build_right(0, 2)
    make_kernel(0, 2, 0, 4)
    pump(ev, 2)
    split_field(2, zg[0, 2])
    split_field(6, zg[0, 6])
    mate_wait(dfy, 2, 1)
    build_right(1, 1)
    make_kernel(1, 1, 0, 4)
    pump(ev, 1)
    mate_wait(dfy, 2, 3)
    build_right(1, 3)
    make_kernel(1, 3, 0, 4)
    pump(ev, 1)
    mate_wait(dfy, 2, 2)
    build_right(1, 2)
    make_kernel(1, 2, 0, 4)
    pump(ev, 2)
    split_field(3, zg[0, 3])
    split_field(5, zg[0, 5])
    timed_early(0)
    pump(ev, 2)
    split_field(4, zg[0, 4])
    dw = send_w(0)
    finish_w(0, dw, False)

    dz = z_ring(1)
    for i, (sl, total) in enumerate(spread(0, None, CHUNKS)):
        q = mk[sl, :] * total + nz[sl, :] * gx[0, 0, sl]
        zg[1, 0, sl] = q
        gx[1, 0, sl] = q
        c = (i % 2) * CHUNKS // 2 + i // 2
        dz["RL"[i % 2], 1, c].start()
    for c in range(CHUNKS // 2):
        dz["R", 1, c + CHUNKS // 2].start()
        dz["L", 1, c].start()
    r0, q = zg[0, 0], zg[1, 0]
    sum_start(0, r0 * r0, r0 * q)
    dx, dx0 = x_ring(1), x_ring(0)
    ring_start(dx, 2)
    ring_start(dx0, 2)
    ev = z_events(dz)
    pump(ev, 3)
    sum_middle(0)
    pump(ev, 7)
    ring_step1(dx, 2, False)
    ring_step1(dx0, 2, False)
    norm0, curv0 = sum_end(0)
    alpha = norm0 / curv0

    def residual_block(k):
        return zg[0, k] - alpha * zg[1, k]

    r1 = residual_block(0)
    sum_start(1, r1 * r1, r1)
    split_field(0, r1)
    for k in (1, 7, 2, 6):
        split_field(k, residual_block(k))
    pump(ev, 2)
    for k in (3, 5):
        split_field(k, residual_block(k))
    timed_early(1)
    pump(ev, 2)
    split_field(4, residual_block(4))
    dw = send_w(1)
    sum_middle(1)
    ring_step2(dx, 2, False)
    ring_step2(dx0, 2, False)
    finish_w(1, dw, False)
    norm1, _ = sum_end(1)
    beta = norm1 / norm0

    def curvature():
        r1 = gx[0, 0] - alpha * gx[1, 0]
        d1 = r1 + beta * gx[0, 0]
        terms = d1 * (p[1, 0] + nz[...] * r1 + beta * gx[1, 0])
        for k in (1, 2, 3):
            terms += p[1, k] * (gx[0, k] - alpha * gx[1, k] + beta * gx[0, k])
        sum_start(2, terms, terms)

    for sl, total in spread(1, curvature, 2):
        r1 = gx[0, 0, sl] - alpha * gx[1, 0, sl]
        res[sl, :] = mk[sl, :] * total + nz[sl, :] * r1 + beta * gx[1, 0, sl]
    curv1, _ = sum_end(2)
    alpha1 = norm1 / curv1
    r0 = gx[0, 0]
    r1 = r0 - alpha * gx[1, 0]
    sol[...] = alpha * r0 + alpha1 * (r1 + beta * r0)
    res[...] = r1 - alpha1 * res[...]

    for d in copies:
        d.wait_send()
    for n in range(3):
        whole(n, 0).wait_send()
        whole(n, 1).wait_send()


def body(targets, features, inv_scales, noise, time_kernel, block_mask):
    vmem = pl.BlockSpec(memory_space=pltpu.VMEM)
    block = jax.ShapeDtypeStruct((ROWS, COLS), F32)
    return pl.pallas_call(
        kernel,
        out_shape=(block, block),
        in_specs=[pl.BlockSpec(memory_space=pl.ANY)] * 6,
        out_specs=(vmem, vmem),
        scratch_shapes=[
            pltpu.VMEM((ROWS, COLS), F32),
            pltpu.VMEM((FEAT, ROWS), F32),
            pltpu.VMEM((1, FEAT), F32),
            pltpu.VMEM((1, ROWS), F32),
            pltpu.VMEM((COLS, NZ * COLS), F32),
            pltpu.VMEM((1, ROWS), jnp.int32),
            pltpu.SemaphoreType.DMA((6,)),
            pltpu.VMEM((2, NZ, ROWS, COLS), F32),
            pltpu.VMEM((2, NX, ROWS, COLS), F32),
            pltpu.VMEM((2, NCORE, NY, ROWS, COLS), F32),
            pltpu.VMEM((NCORE, NY, FEAT, ROWS), F32),
            pltpu.VMEM((NX, FEAT, ROWS), F32),
            pltpu.VMEM((NX * ROWS, DEPTH), BF16),
            pltpu.VMEM((DEPTH, 8 * ROWS), BF16),
            pltpu.VMEM((NX * ROWS, 16 * ROWS), BF16),
            pltpu.VMEM((8 * ROWS, 2 * COLS), BF16),
            pltpu.VMEM((ROWS, 2 * NZ * COLS), BF16),
            pltpu.VMEM((2 * COLS, NZ * COLS), BF16),
            pltpu.VMEM((2, NX, ROWS, COLS), F32),
            pltpu.VMEM((2, 1, ROWS, COLS), F32),
            pltpu.VMEM((2, 2, ROWS, COLS), F32),
            pltpu.VMEM((ROWS, COLS), F32),
            pltpu.VMEM((ROWS, COLS), F32),
            pltpu.VMEM((3, 2, 2, COLS), F32),
            pltpu.VMEM((3, PLANE - 1, 2, COLS), F32),
            pltpu.VMEM((3, NZ - 1, 2, COLS), F32),
            pltpu.SemaphoreType.DMA((NSEM,)),
            pltpu.SemaphoreType.DMA((NSEM,)),
            pltpu.SemaphoreType.DMA((3, 2)),
            pltpu.SemaphoreType.DMA((3, 2)),
        ],
        compiler_params=pltpu.CompilerParams(
            collective_id=0, has_side_effects=True, vmem_limit_bytes=67043328
        ),
    )(
        targets, features.T, inv_scales.reshape(1, FEAT), noise.reshape(1, ROWS), time_kernel, block_mask.T
    )


def solution(mesh):
    return jax.shard_map(
        body,
        mesh=mesh,
        in_specs=(P("cfg", "tm"), P("cfg", None), P(), P("cfg"), P("tm", None), P("cfg", "tm")),
        out_specs=(P("cfg", "tm"), P("cfg", "tm")),
        check_vma=False,
    )
```
